256 devices in a mesh: gx: 4 (over y_lo, core), gy: 64 (over y_hi, x, z).
Axes of the slice: x: 4, y: 4 (y_hi: 2, y_lo: 2; y = y_hi * 2 + y_lo), z: 8, core: 2. Of those that a mesh axis runs over, the one named last changes fastest.
Arguments:
- hidden: bfloat16 [8192, 2048], P('gy', 'gx'), may hold values from -6 to 6
- segment_ids: int32 [8192], replicated, may hold values from 0 to 31, never falling along the last dimension, each value on 1 to 4352 neighbouring positions
- expert_ids: int32 [8192, 6], P('gy'), may hold values from 0 to 63, all different within a row; in each aligned block of 128 rows (0 to 127, 128 to 255, ...) at most 15 rows name the same one
- route_weight: float32 [8192, 6], P('gy'), may hold values from 0.1 to 1
- attn_gain: float32 [2048], replicated, may hold values from 0.1 to 1.9
- kv_gain: float32 [512], replicated, may hold values from 0.1 to 1.9
- ffn_gain: float32 [2048], replicated, may hold values from 0.1 to 1.9
- w_q: bfloat16 [2048, 3072], P('gy', 'gx'), may hold values from -2 to 2
- w_kv_a: bfloat16 [2048, 576], P('gy', 'gx'), may hold values from -0.125 to 0.125
- w_kv_b: bfloat16 [512, 4096], P('gy', 'gx'), may hold values from -0.25 to 0.25
- w_o: bfloat16 [2048, 2048], P('gx', 'gy'), may hold values from -0.125 to 0.125
- w_gate: bfloat16 [64, 2048, 1408], P('gy', None, 'gx'), may hold values from -0.125 to 0.125
- w_up: bfloat16 [64, 2048, 1408], P('gy', None, 'gx'), may hold values from -0.125 to 0.125
- w_down: bfloat16 [64, 1408, 2048], P('gy', 'gx'), may hold values from -0.15625 to 0.15625
- page_table: int32 [512], P(('gx', 'gy')), may hold values from 0 to 511, each once
Outputs:
- output: bfloat16 [8192, 2048], P('gy', 'gx')
- latent_cache: bfloat16 [512, 16, 576], P(('gx', 'gy'))
The draws below stay inside these ranges and needn't reach their ends.
Inputs may be any that keep to these rules, and one draw needn't show every extreme that they name: `segment_ids`: never falling along the stream; every prompt has 1 to 4352 tokens and one has exactly 4352. `expert_ids`: a token names 6 different experts; among the rows of one index of gy no expert is named by more than 15 rows, and in some of them one expert is named by exactly 15. `page_table`: a permutation of the stream's pages.
All inputs are finite; a program needn't handle non-finite values.
Results may differ from the reference program's by a relative error of at most 0.014.
The reference program's roundings to bfloat16 on the way count: a program that leaves them out, or rounds other values in their place, can miss the bound.
Values may be sent and summed in bfloat16 or wider, within the bound.
No kernel may reach another device: no remote copies, remote signals or barrier semaphores. Data moves between devices by JAX's collectives and lax.ppermute only.
A program may use at most 128 MiB of HBM per device.

```python
import math
import jax
import jax.numpy as jnp
import numpy as np
from jax import lax

D = 2048
HEADS = 16
NOPE = 128
ROPE = 64
VDIM = 128
RANK = 512
FF = 1408
TOP = 6
EXPERTS = 64
ROWS_GY = 128
TOKENS = 8192
SEGS = 32
LONGEST = 4352
CAP = 15
QUART = 352
PAGE = 16
PAGES = 512
N_GY = 64


def draw_w_q(key, part):
    values = jnp.clip(jax.random.normal(key, (D, HEADS * (NOPE + ROPE)), jnp.float32), -4.0, 4.0) * D ** (-0.5)
    values = jnp.clip(values, -2.0, 2.0)
    return values.astype(jnp.bfloat16)


def block_levels(stream_key, dims, cuts, least, top_value):
    loudness, own = 1.0, jax.random.fold_in(stream_key, 6)
    for position, blocks in cuts:
        draws = jnp.exp(jax.random.uniform(jax.random.fold_in(own, position), (blocks,), jnp.float32, least / len(cuts), top_value / len(cuts)))
        loudness = loudness * jnp.repeat(draws, dims[position] // blocks).reshape([-1 if axis == position else 1 for axis in range(len(dims))])
    return loudness


def split_up(number_of, total, reach, slope):
    weights = [(1 << 20) // math.isqrt(rank ** slope) + 1 for rank in range(2, number_of + 1)]
    rest, given = total - reach - (number_of - 1), [1] * (number_of - 1)
    while rest > 0:
        movable = [i for i in range(number_of - 1) if given[i] < reach]
        whole, remaining = sum([weights[i] for i in movable]), rest
        for i in movable:
            more = min(reach - given[i], max(1, remaining * weights[i] // whole), rest)
            given[i] = given[i] + more
            rest = rest - more
    return np.array([reach] + given)


def ragged_sizes(rng, count, total, limit, slope):
    if count == 2:
        one = jax.random.randint(rng, (), max(1, total - limit), min(limit, total - 1) + 1)
        return jnp.stack([one, total - one])
    tallies = jnp.asarray(split_up(count, total, limit, slope), jnp.int32)
    couples = (count - 1) // 2
    donor, receiver = tallies[1:1 + 2 * couples:2], tallies[2:2 + 2 * couples:2]
    slack = jnp.minimum(donor - 1, limit - receiver)
    passed = jax.random.randint(jax.random.fold_in(rng, 1), (couples,), 0, 1 << 20) % (slack + 1)
    tallies = tallies.at[1:1 + 2 * couples:2].set(donor - passed).at[2:2 + 2 * couples:2].set(receiver + passed)
    return tallies[jax.random.permutation(jax.random.fold_in(rng, 2), count)]


def assign_block(own_key, own, number, rows, count, top, most, slope):
    sequence = jax.random.permutation(own_key, count)
    heavy_load, ordinary = load_shares(count, rows * top, most, slope, True), load_shares(count, rows * top, most, slope, False)
    places = jnp.arange(count)

    def named(tallies, rotation):
        used = int((tallies > 0).sum())
        fixed = max(1, used // 4)
        shifted = fixed + (places - fixed + rotation * (used - fixed)) % max(1, count - fixed)
        return jnp.zeros((count,), jnp.int32).at[sequence[jnp.where(places < fixed, places, shifted)]].set(jnp.asarray(tallies, jnp.int32))

    tallies = jnp.where(number % 4 == 0, named(heavy_load, number // 4), named(ordinary, number - number // 4 - 1))
    mixed = jax.random.permutation(jax.random.fold_in(own, 3), count)
    donor, taker = mixed[0:count // 2 * 2:2], mixed[1:count // 2 * 2:2]
    margin = jnp.minimum(tallies[donor] - 1, most - tallies[taker]) // 2
    margin = jnp.where((donor == sequence[0]) | (taker == sequence[0]) | (tallies[taker] == 0), 0, jnp.maximum(margin, 0))
    shifted = jax.random.randint(jax.random.fold_in(own, 4), (count // 2,), 0, 1 << 20) % (margin + 1)
    tallies = tallies.at[donor].add(-shifted).at[taker].add(shifted)
    labels = jnp.searchsorted(jnp.cumsum(tallies), jnp.arange(rows * top), side="right").astype(jnp.int32)
    listing = labels.reshape(top, rows).T
    listing = listing[jax.random.permutation(jax.random.fold_in(own, 1), rows)]
    rotation = jax.random.randint(jax.random.fold_in(own, 2), (rows, 1), 0, top)
    return jnp.take_along_axis(listing, (jnp.arange(top)[None, :] + rotation) % top, axis=1)


def load_shares(count, total, reach, slope, full):
    portions = [(1 << 20) // math.isqrt(standing ** slope) + 1 for standing in range(1, count + 1)]
    largest = reach if full else min(reach, max(-(-total // count), total * portions[0] // sum(portions)))
    least = 1 if total - largest >= count - 1 else 0
    holding, surplus = [largest] + [least] * (count - 1), total - largest - least * (count - 1)
    while surplus > 0:
        candidates = [i for i in range(1, count) if holding[i] < largest] or [i for i in range(1, count) if holding[i] < reach]
        mass, left = sum([portions[i] for i in candidates]), surplus
        for i in candidates:
            extra = min(reach - holding[i], max(1, left * portions[i] // mass), surplus)
            holding[i] = holding[i] + extra
            surplus = surplus - extra
    return np.array(holding)


def gaussian(own_key, dims, spread, bound, pieces=(), kind=jnp.bfloat16):
    entries = jax.random.normal(own_key, dims, jnp.float32) * spread
    if len(pieces) > 0:
        entries = block_levels(own_key, dims, pieces, -0.22, 0.18) * entries
    return jnp.clip(entries, min=-bound, max=bound).astype(kind)


def setup_inputs(seed: int = 0) -> dict:
    streams_of = jax.random.split(jax.random.key(seed), 16)
    hidden = gaussian(streams_of[0], (TOKENS, D), 1.0, 6.0, ((0, 64), (1, 4)))
    segment_ids = jnp.searchsorted(jnp.cumsum(ragged_sizes(streams_of[1], SEGS, TOKENS, LONGEST, 2)), jnp.arange(TOKENS), side="right").astype(jnp.int32)
    expert_ids_keys = jax.random.split(jax.random.fold_in(streams_of[2], 1), TOKENS // ROWS_GY)
    expert_ids_turns = jax.random.permutation(jax.random.fold_in(streams_of[2], 3), TOKENS // ROWS_GY)
    expert_ids = jax.vmap(lambda own, number: assign_block(jax.random.fold_in(streams_of[2], 2), own, number, ROWS_GY, EXPERTS, TOP, CAP, 2))(expert_ids_keys, expert_ids_turns).reshape((TOKENS, TOP))
    route_weight = jnp.clip(jnp.exp(math.log(1.0) - 2.3025851 * jax.random.uniform(streams_of[3], (TOKENS, TOP), jnp.float32) ** block_levels(streams_of[3], (TOKENS, TOP), ((0, 64),), -0.2, 0.2)), 0.1, 1.0)
    attn_gain = jnp.clip(1.0 + 0.18 * jax.random.normal(streams_of[4], (D,), jnp.float32), 0.1, 1.9)
    kv_gain = jnp.clip(1.0 + 0.18 * jax.random.normal(streams_of[5], (RANK,), jnp.float32), 0.1, 1.9)
    ffn_gain = jnp.clip(1.0 + 0.18 * jax.random.normal(streams_of[6], (D,), jnp.float32), 0.1, 1.9)
    w_q = draw_w_q(jax.random.fold_in(streams_of[15], 71), 0)
    w_kv_a = gaussian(streams_of[8], (D, RANK + ROPE), D ** -0.5, 0.125, ((0, 64), (1, 4)))
    w_kv_b = gaussian(streams_of[9], (RANK, HEADS * (NOPE + VDIM)), RANK ** -0.5, 0.25, ((0, 64), (1, 4)))
    w_o = gaussian(streams_of[10], (HEADS * VDIM, D), (HEADS * VDIM) ** -0.5, 0.125, ((0, 4), (1, 64)))
    w_gate = gaussian(streams_of[11], (EXPERTS, D, FF), D ** -0.5, 0.125, ((0, 64), (2, 4)))
    w_up = gaussian(streams_of[12], (EXPERTS, D, FF), D ** -0.5, 0.125, ((0, 64), (2, 4)))
    w_down = gaussian(streams_of[13], (EXPERTS, FF, D), FF ** -0.5, 0.15625, ((0, 64), (1, 4)))
    page_table = jax.random.permutation(streams_of[14], PAGES).astype(jnp.int32)
    return {"hidden": hidden, "segment_ids": segment_ids, "expert_ids": expert_ids, "route_weight": route_weight, "attn_gain": attn_gain, "kv_gain": kv_gain, "ffn_gain": ffn_gain, "w_q": w_q, "w_kv_a": w_kv_a, "w_kv_b": w_kv_b, "w_o": w_o, "w_gate": w_gate, "w_up": w_up, "w_down": w_down, "page_table": page_table}


eps = 1e-06
masked_score = -1e+30

def norm_rows(values, gain):
    mean_sq = lax.optimization_barrier(jnp.mean(values * values, axis=-1, keepdims=True))
    return values * lax.rsqrt(mean_sq + eps) * gain

def angle_table(positions, width):
    exponents = jnp.arange(width // 2, dtype=jnp.float32) * (2.0 / width)
    freqs = jnp.power(10000.0, -exponents)
    return positions.astype(jnp.float32)[:, None] * freqs[None, :]

def rotate(values, angles):
    half = values.shape[-1] // 2
    first = values[..., :half]
    second = values[..., half:]
    cosine = jnp.cos(angles)
    sine = jnp.sin(angles)
    return jnp.concatenate([first * cosine - second * sine, second * cosine + first * sine], axis=-1)

def reference(hidden, segment_ids, expert_ids, route_weight, attn_gain, kv_gain, ffn_gain, w_q, w_kv_a, w_kv_b, w_o, w_gate, w_up, w_down, page_table):
    token_count = hidden.shape[0]
    positions = jnp.arange(token_count, dtype=jnp.int32)
    prompt_start = jnp.searchsorted(segment_ids, segment_ids, side='left').astype(jnp.int32)
    local_positions = (positions - prompt_start).astype(jnp.int32)
    normed = norm_rows(hidden.astype(jnp.float32), attn_gain).astype(jnp.bfloat16)
    query = jnp.dot(normed, w_q, preferred_element_type=jnp.float32).reshape(token_count, HEADS, NOPE + ROPE)
    kv_raw = jnp.dot(normed, w_kv_a, preferred_element_type=jnp.float32)
    angles = angle_table(local_positions, ROPE)
    keys = jnp.concatenate([norm_rows(kv_raw[:, :RANK], kv_gain), rotate(kv_raw[:, RANK:], angles)], axis=1).astype(jnp.bfloat16)
    latent_cache = keys.reshape(token_count // PAGE, PAGE, RANK + ROPE)[page_table]
    scale = (NOPE + ROPE) ** (-0.5)
    expand = w_kv_b.reshape(RANK, HEADS, NOPE + VDIM).astype(jnp.float32)
    q_nope = query[:, :, :NOPE].astype(jnp.bfloat16)
    absorbed = (jnp.einsum('thn,rhn->htr', q_nope.astype(jnp.float32), expand[:, :, :NOPE]) * scale).astype(jnp.bfloat16)
    rotated = (rotate(query[:, :, NOPE:], angles[:, None, :]) * scale).astype(jnp.bfloat16)
    queries = jnp.concatenate([absorbed, jnp.transpose(rotated, (1, 0, 2))], axis=2)
    block = min(512, token_count)
    block_count = token_count // block

    def attend_block(block_index):
        q_start = block_index.astype(jnp.int32) * block
        q_block = lax.dynamic_slice_in_dim(queries, q_start, block, 1).astype(jnp.float32)
        q_segments = lax.dynamic_slice_in_dim(segment_ids, q_start, block)
        q_positions = q_start + jnp.arange(block, dtype=jnp.int32)

        def scored(key_index):
            k_start = key_index * block
            key_block = lax.dynamic_slice_in_dim(keys, k_start, block, 0).astype(jnp.float32)
            k_segments = lax.dynamic_slice_in_dim(segment_ids, k_start, block)
            k_positions = k_start + jnp.arange(block, dtype=jnp.int32)
            allowed = (q_segments[:, None] == k_segments[None, :]) & (k_positions[None, :] <= q_positions[:, None])
            scores = jnp.einsum('htc,sc->hts', q_block, key_block)
            return (jnp.where(allowed[None], scores, masked_score), allowed, key_block)

        def needed(key_index):
            k_start = key_index * block
            last_segment = lax.dynamic_index_in_dim(segment_ids, k_start + block - 1, keepdims=False)
            return (k_start <= q_start + block - 1) & (last_segment >= q_segments[0])

        def max_step(key_index, best):
            key_index = jnp.asarray(key_index).astype(jnp.int32)
            return lax.cond(needed(key_index), lambda inner: jnp.maximum(inner, lax.optimization_barrier(jnp.max(scored(key_index)[0], axis=-1))), lambda inner: inner, best)
        best = lax.fori_loop(0, block_count, max_step, jnp.full((HEADS, block), masked_score, jnp.float32))

        def sum_step(key_index, state):
            key_index = jnp.asarray(key_index).astype(jnp.int32)

            def accumulate(inner):
                total, accum = inner
                scores, allowed, key_block = scored(key_index)
                exponent = jnp.where(allowed[None], jnp.exp(scores - best[..., None]), 0.0)
                weights = lax.optimization_barrier(exponent.astype(jnp.bfloat16)).astype(jnp.float32)
                return (total + lax.optimization_barrier(jnp.sum(exponent, axis=-1)), accum + jnp.einsum('hts,sc->htc', weights, key_block[:, :RANK]))
            return lax.cond(needed(key_index), accumulate, lambda inner: inner, state)
        total, accum = lax.fori_loop(0, block_count, sum_step, (jnp.zeros((HEADS, block), jnp.float32), jnp.zeros((HEADS, block, RANK), jnp.float32)))
        return (accum / total[..., None]).astype(jnp.bfloat16)
    mixed = lax.map(attend_block, jnp.arange(block_count, dtype=jnp.int32))
    mixed = jnp.transpose(mixed, (1, 0, 2, 3)).reshape(HEADS, token_count, RANK)
    heads_out = jnp.einsum('htc,chv->thv', mixed.astype(jnp.float32), expand[:, :, NOPE:]).astype(jnp.bfloat16).reshape(token_count, HEADS * VDIM)
    head_total = jnp.dot(heads_out, w_o, preferred_element_type=jnp.float32)
    residual = (hidden.astype(jnp.float32) + head_total).astype(jnp.bfloat16)
    ffn_in = norm_rows(residual.astype(jnp.float32), ffn_gain).astype(jnp.bfloat16)
    pair_count = token_count * TOP
    flat_ids = expert_ids.reshape(-1).astype(jnp.int32)
    order = jnp.argsort(flat_ids * pair_count + jnp.arange(pair_count, dtype=jnp.int32)).astype(jnp.int32)
    counts = lax.optimization_barrier(jnp.sum((flat_ids[:, None] == jnp.arange(EXPERTS, dtype=jnp.int32)[None, :]).astype(jnp.int32), axis=0))
    offsets = (jnp.cumsum(counts) - counts).astype(jnp.int32)
    slot_total = N_GY * CAP
    padded = jnp.concatenate([order, jnp.zeros((slot_total,), jnp.int32)])
    flat_weight = route_weight.reshape(-1)
    block_total = FF // QUART

    def expert_step(moe, inputs):
        gate_weight, up_weight, down_weight, offset, count = inputs
        pairs = lax.dynamic_slice_in_dim(padded, offset.astype(jnp.int32), slot_total)
        valid = jnp.arange(slot_total, dtype=jnp.int32) < count
        token_index = pairs // TOP
        chosen = ffn_in[token_index]
        gate = jnp.dot(chosen, gate_weight, preferred_element_type=jnp.float32)
        upper = jnp.dot(chosen, up_weight, preferred_element_type=jnp.float32)
        active = (jax.nn.silu(gate) * upper).astype(jnp.bfloat16)
        parts = jnp.einsum('sqf,qfd->sqd', active.reshape(slot_total, block_total, QUART).astype(jnp.float32), down_weight.reshape(block_total, QUART, D).astype(jnp.float32))
        parts = lax.optimization_barrier(parts.astype(jnp.bfloat16)).astype(jnp.float32)
        scaled = jnp.where(valid, flat_weight[pairs], 0.0)
        combined = lax.optimization_barrier(jnp.sum(parts, axis=1)) * scaled[:, None]
        return (moe.at[token_index].add(combined), None)
    moe, unused = lax.scan(expert_step, jnp.zeros((token_count, D), jnp.float32), (w_gate, w_up, w_down, offsets, counts))
    output = (residual.astype(jnp.float32) + moe).astype(jnp.bfloat16)
    return (output, latent_cache)
```

```python
import jax
import jax.numpy as jnp
from jax import lax
from jax.experimental import pallas as pl
from jax.experimental.pallas import tpu as pltpu
from jax.sharding import Mesh, PartitionSpec as P

NOPE = 128
ROPE = 64
VDIM = 128
RANK = 512
PAGE = 16
KEY = RANK + ROPE

GX = ("yl", "c")
GY = ("yh", "x", "z")
YL, CORES, YH, XS, ZS = 2, 2, 2, 4, 8
GROUPS = YH * XS * ZS
PARTS = YL * CORES
SLOTS = 16
SWAP = [(0, 1), (1, 0)]

eps = 1e-06
masked_score = -1e30


def norm_rows(values, gain):
    mean_sq = jnp.mean(values * values, axis=-1, keepdims=True)
    return values * lax.rsqrt(mean_sq + eps) * gain


def angle_table(positions, width):
    exponents = jnp.arange(width // 2, dtype=jnp.float32) * (2.0 / width)
    freqs = jnp.power(10000.0, -exponents)
    return positions.astype(jnp.float32)[:, None] * freqs[None, :]


def rotate(values, cosine, sine):
    half = values.shape[-1] // 2
    first = values[..., :half]
    second = values[..., half:]
    return jnp.concatenate(
        [first * cosine - second * sine, second * cosine + first * sine], axis=-1
    )


def shift(values, axis, size, step):
    return lax.ppermute(values, axis, [(i, (i + step) % size) for i in range(size)])


def swap(values, axis):
    return lax.ppermute(values, axis, SWAP)


def spread(values, axis, size):
    blocks = jnp.broadcast_to(values[None], (size,) + values.shape)
    return lax.all_to_all(blocks, axis, split_axis=0, concat_axis=0, tiled=True)


def attention_kernel(
    meta, q_ref, qlo_ref, qpos_ref, a_own, a_oth, b_own, b_oth, wuv_ref, wo_ref, out_ref,
    best, total, accum, heads,
):
    step = pl.program_id(0)
    kmin, kmax, core = meta[16], meta[17], meta[18]

    @pl.when(step == 0)
    def _():
        best[...] = jnp.full_like(best, masked_score)
        total[...] = jnp.zeros_like(total)
        accum[...] = jnp.zeros_like(accum)

    def block(base, colour, own_ref, oth_ref):
        @pl.when((base <= kmax) & (base + 1023 >= kmin))
        def _():
            queries = q_ref[...]
            lo, hi = qlo_ref[...], qpos_ref[...]
            row = lax.broadcasted_iota(jnp.int32, (1, 256), 1)
            place = base + (row // 32) * 128 + row % 32 + colour * 32
            scores, masks = [], []
            for ref, side in ((own_ref, core), (oth_ref, 1 - core)):
                keys = ref[0]
                raw = lax.dot_general(
                    queries, keys, (((1,), (1,)), ((), ())), preferred_element_type=jnp.float32
                )
                where = place + side * 64
                mask = (where >= lo) & (where <= hi)
                scores.append(jnp.where(mask, raw, masked_score))
                masks.append(mask)
            old = best[...]
            new = jnp.maximum(
                old,
                jnp.maximum(
                    jnp.max(scores[0], axis=-1, keepdims=True),
                    jnp.max(scores[1], axis=-1, keepdims=True),
                ),
            )
            alpha = jnp.exp(old - new)
            best[...] = new
            grown = total[...] * alpha
            fresh = accum[...] * alpha
            for ref, score, mask in ((own_ref, scores[0], masks[0]), (oth_ref, scores[1], masks[1])):
                weight = jnp.where(mask, jnp.exp(score - new), 0.0)
                grown = grown + jnp.sum(weight, axis=-1, keepdims=True)
                fresh = fresh + jnp.dot(
                    weight.astype(jnp.bfloat16), ref[0, :, :RANK],
                    preferred_element_type=jnp.float32,
                )
            total[...] = grown
            accum[...] = fresh

    block(meta[step], 0, a_own, a_oth)
    block(meta[8 + step], 1, b_own, b_oth)

    @pl.when(step == pl.num_programs(0) - 1)
    def _():
        rows = out_ref.shape[0]
        mixed = (accum[...] / total[...]).astype(jnp.bfloat16)
        for h in range(wuv_ref.shape[0]):
            heads[:, h * VDIM : (h + 1) * VDIM] = jnp.dot(
                mixed[h * rows : (h + 1) * rows], wuv_ref[h], preferred_element_type=jnp.float32
            ).astype(jnp.bfloat16)
        out_ref[...] = lax.dot_general(
            heads[...], wo_ref[...], (((1,), (1,)), ((), ())), preferred_element_type=jnp.float32
        )


def attention(meta, queries, qlo, qpos, keys, w_uv, w_o):
    head_rows = queries.shape[0]
    rows = head_rows // w_uv.shape[0]

    def whole(shape):
        return pl.BlockSpec(shape, lambda i, m: (0,) * len(shape))

    key_spec = pl.BlockSpec((1, 256, KEY), lambda i, m: (i, 0, 0))
    return pl.pallas_call(
        attention_kernel,
        out_shape=jax.ShapeDtypeStruct((rows, w_o.shape[0]), jnp.float32),
        grid_spec=pltpu.PrefetchScalarGridSpec(
            num_scalar_prefetch=1,
            grid=(8,),
            in_specs=[
                whole(queries.shape), whole(qlo.shape), whole(qpos.shape),
                key_spec, key_spec, key_spec, key_spec,
                whole(w_uv.shape), whole(w_o.shape),
            ],
            out_specs=whole((rows, w_o.shape[0])),
            scratch_shapes=[
                pltpu.VMEM((head_rows, 1), jnp.float32),
                pltpu.VMEM((head_rows, 1), jnp.float32),
                pltpu.VMEM((head_rows, RANK), jnp.float32),
                pltpu.VMEM((rows, w_uv.shape[0] * VDIM), jnp.bfloat16),
            ],
        ),
        cost_estimate=pl.CostEstimate(
            flops=9_000_000_000, bytes_accessed=16_000_000, transcendentals=4_000_000
        ),
        compiler_params=pltpu.CompilerParams(
            dimension_semantics=("arbitrary",), vmem_limit_bytes=40 << 20
        ),
    )(meta, queries, qlo, qpos, *keys, w_uv, w_o)


def expert_kernel(order, x0, x1, x2, x3, wg_ref, wu_ref, wd_ref, o0, o1, o2, o3):
    share = x0.shape[1]
    gate = jnp.zeros((x0.shape[0], wg_ref.shape[1]), jnp.float32)
    upper = gate
    starts = [pl.multiple_of(order[j] * share, share) for j in range(4)]
    for start, ref in zip(starts, (x0, x1, x2, x3)):
        piece = ref[...]
        gate = gate + jnp.dot(
            piece, wg_ref[pl.ds(start, share), :], preferred_element_type=jnp.float32
        )
        upper = upper + jnp.dot(
            piece, wu_ref[pl.ds(start, share), :], preferred_element_type=jnp.float32
        )
    active = (gate / (1.0 + jnp.exp(-gate)) * upper).astype(jnp.bfloat16)
    for start, ref in zip(starts, (o0, o1, o2, o3)):
        ref[...] = jnp.dot(
            active, wd_ref[:, pl.ds(start, share)], preferred_element_type=jnp.float32
        ).astype(jnp.bfloat16)


def experts(order, pieces, w_gate, w_up, w_down):
    count, share = pieces[0].shape
    tile = 256

    def whole(shape):
        return pl.BlockSpec(shape, lambda i, m: (0,) * len(shape))

    row_spec = pl.BlockSpec((tile, share), lambda i, m: (i, 0))
    return pl.pallas_call(
        expert_kernel,
        out_shape=[jax.ShapeDtypeStruct((count, share), jnp.bfloat16)] * 4,
        grid_spec=pltpu.PrefetchScalarGridSpec(
            num_scalar_prefetch=1,
            grid=(count // tile,),
            in_specs=[row_spec] * 4
            + [whole(w_gate.shape), whole(w_up.shape), whole(w_down.shape)],
            out_specs=[row_spec] * 4,
        ),
        cost_estimate=pl.CostEstimate(
            flops=4_400_000_000, bytes_accessed=13_000_000, transcendentals=400_000
        ),
        compiler_params=pltpu.CompilerParams(
            dimension_semantics=("arbitrary",), vmem_limit_bytes=40 << 20
        ),
    )(order, *pieces, w_gate, w_up, w_down)


def shards(
    hidden, segment_ids, expert_ids, route_weight, attn_gain, kv_gain, ffn_gain,
    w_q, w_kv_a, w_kv_b, w_o, w_gate, w_up, w_down, page_table,
):
    row_count, share = hidden.shape
    yl, core = lax.axis_index("yl"), lax.axis_index("c")
    yh, x, z = (lax.axis_index(name) for name in GY)
    row_start = ((yh * XS + x) * ZS + z) * row_count
    head_count = w_q.shape[1] // (NOPE + ROPE)
    depth = w_q.shape[0]

    expand_rows = w_kv_b.shape[0]
    local_expand = (
        w_kv_b.reshape(expand_rows, head_count, NOPE + VDIM)
        .transpose(1, 0, 2)
        .reshape(expand_rows * head_count, NOPE + VDIM)
    )
    packed = jnp.concatenate([w_q, local_expand, w_o.T], axis=1)
    weights = lax.all_gather(packed, GY, axis=0, tiled=True)
    tail_cols = w_kv_a.shape[1] - 128
    latent_packed = jnp.concatenate(
        [w_kv_a[:, :128], w_kv_a[:, 128:].reshape(depth * tail_cols // 128, 128)], axis=0
    )
    latent_all = spread(latent_packed, GY, GROUPS)
    latent_main = latent_all[:, :depth].reshape(GROUPS * depth, 128)
    latent_tail = latent_all[:, depth:].reshape(GROUPS * depth, tail_cols)

    positions = row_start + jnp.arange(row_count, dtype=jnp.int32)
    own_segments = lax.dynamic_slice_in_dim(segment_ids, row_start, row_count)
    prompt_start = jnp.sum(
        (segment_ids[None, :] < own_segments[:, None]).astype(jnp.int32), axis=1
    )
    angles = angle_table(positions - prompt_start, ROPE)
    cosine, sine = jnp.cos(angles), jnp.sin(angles)

    full_rows = lax.all_gather(hidden, GX, axis=1, tiled=True)
    normed = norm_rows(full_rows.astype(jnp.float32), attn_gain).astype(jnp.bfloat16)

    kv_part = jnp.concatenate(
        [
            jnp.dot(normed, latent_main, preferred_element_type=jnp.float32),
            jnp.dot(normed, latent_tail, preferred_element_type=jnp.float32),
        ],
        axis=1,
    )
    kv_raw = lax.all_gather(kv_part, GX, axis=1, tiled=True)
    half = row_count // CORES
    kv_half = lax.dynamic_slice_in_dim(kv_raw, core * half, half)
    keys = jnp.concatenate(
        [
            norm_rows(kv_half[:, :RANK], kv_gain),
            rotate(
                kv_half[:, RANK:],
                lax.dynamic_slice_in_dim(cosine, core * half, half),
                lax.dynamic_slice_in_dim(sine, core * half, half),
            ),
        ],
        axis=1,
    ).astype(jnp.bfloat16)
    along_z = spread(keys, "z", ZS)
    quarter = half // 2
    a0 = along_z[:, :quarter].reshape(1, ZS * quarter, KEY)
    b0 = along_z[:, quarter:].reshape(1, ZS * quarter, KEY)
    b1 = jnp.concatenate([b0, swap(b0, "yh")], axis=0)
    a1 = jnp.concatenate([a0] + [shift(a0, "x", XS, k) for k in range(1, XS)], axis=0)
    a_own = jnp.concatenate([a1, swap(a1, "yh")], axis=0)
    b_own = jnp.concatenate([b1] + [shift(b1, "x", XS, k) for k in range(1, XS)], axis=0)
    a_oth, b_oth = swap(a_own, "c"), swap(b_own, "c")
    steps = jnp.arange(8, dtype=jnp.int32)
    base_a = ((yh ^ (steps // 4)) * XS + (x - steps % 4) % XS) * (ZS * row_count)
    base_b = ((yh ^ (steps % 2)) * XS + (x - steps // 2) % XS) * (ZS * row_count)
    meta = jnp.concatenate(
        [
            base_a, base_b,
            jnp.stack([prompt_start[0], row_start + row_count - 1, core]).astype(jnp.int32),
        ]
    ).astype(jnp.int32)

    pages = []
    for i in range(page_table.shape[0]):
        page = page_table[i]
        group, inside = page // (row_count // PAGE), page % (row_count // PAGE)
        far_yh, far_x = (group // (XS * ZS)) ^ yh, (x - (group // ZS) % XS) % XS
        start = (group % ZS) * quarter + (inside % 2) * PAGE
        is_own = inside // 4 == core
        index_a, index_b = far_yh * XS + far_x, far_x * YH + far_yh
        size = (1, PAGE, KEY)
        from_a = jnp.where(
            is_own,
            lax.dynamic_slice(a_own, (index_a, start, 0), size),
            lax.dynamic_slice(a_oth, (index_a, start, 0), size),
        )
        from_b = jnp.where(
            is_own,
            lax.dynamic_slice(b_own, (index_b, start, 0), size),
            lax.dynamic_slice(b_oth, (index_b, start, 0), size),
        )
        pages.append(jnp.where((inside % 4) // 2 == 0, from_a, from_b))
    latent_cache = jnp.concatenate(pages, axis=0)

    q_cols = w_q.shape[1]
    expand = (
        weights[:, q_cols : q_cols + NOPE + VDIM]
        .reshape(GROUPS, head_count, expand_rows, NOPE + VDIM)
        .transpose(1, 0, 2, 3)
        .reshape(head_count, RANK, NOPE + VDIM)
    )
    out_rows = weights[:, q_cols + NOPE + VDIM :]
    scale = (NOPE + ROPE) ** (-0.5)
    query = jnp.dot(normed, weights[:, :q_cols], preferred_element_type=jnp.float32).reshape(
        row_count, head_count, NOPE + ROPE
    )
    q_nope = query[:, :, :NOPE].astype(jnp.bfloat16)
    absorbed = (
        jnp.einsum("thn,hrn->htr", q_nope, expand[:, :, :NOPE], preferred_element_type=jnp.float32)
        * scale
    ).astype(jnp.bfloat16)
    rotated = (
        rotate(query[:, :, NOPE:], cosine[:, None, :], sine[:, None, :]) * scale
    ).astype(jnp.bfloat16)
    queries = jnp.concatenate([absorbed, jnp.transpose(rotated, (1, 0, 2))], axis=2).reshape(
        head_count * row_count, KEY
    )
    qlo = jnp.tile(prompt_start.astype(jnp.int32), head_count)[:, None]
    qpos = jnp.tile(positions, head_count)[:, None]
    head_terms = attention(
        meta, queries, qlo, qpos, (a_own, a_oth, b_own, b_oth), expand[:, :, NOPE:], out_rows
    )

    term_blocks = head_terms.reshape(row_count, PARTS, share).transpose(1, 0, 2)
    head_sum = jnp.sum(
        lax.all_to_all(term_blocks, GX, split_axis=0, concat_axis=0, tiled=True), axis=0
    )
    residual = (hidden.astype(jnp.float32) + head_sum).astype(jnp.bfloat16)
    wide = residual.astype(jnp.float32)
    squares = lax.all_gather(jnp.sum(wide * wide, axis=1)[None], GX, axis=0, tiled=True)
    mean_sq = jnp.sum(squares, axis=0)[:, None] * (1.0 / (share * PARTS))
    own_gain = lax.dynamic_slice_in_dim(ffn_gain, (yl * CORES + core) * share, share)
    ffn_in = (wide * lax.rsqrt(mean_sq + eps) * own_gain).astype(jnp.bfloat16)

    top_count = expert_ids.shape[1]
    expert_range = jnp.arange(GROUPS, dtype=jnp.int32)
    chosen = (expert_ids[:, :, None] == expert_range).astype(jnp.float32)
    named = jnp.sum(chosen, axis=1)
    earlier = (
        jnp.arange(row_count)[:, None] > jnp.arange(row_count)[None, :]
    ).astype(jnp.float32)
    before = jnp.dot(earlier, named, preferred_element_type=jnp.float32)
    ranks = jnp.sum(chosen * before[:, None, :], axis=2).astype(jnp.int32)
    slots = expert_ids * SLOTS + ranks
    slot_range = jnp.arange(GROUPS * SLOTS, dtype=jnp.int32)
    pick = jnp.zeros((GROUPS * SLOTS, row_count), jnp.bool_)
    blend = jnp.zeros((row_count, GROUPS * SLOTS), jnp.float32)
    for k in range(top_count):
        pick = pick | (slot_range[:, None] == slots[:, k][None, :])
        blend = blend + jnp.where(
            slots[:, k][:, None] == slot_range[None, :], route_weight[:, k][:, None], 0.0
        )
    outgoing = jnp.dot(
        pick.astype(jnp.bfloat16), ffn_in, preferred_element_type=jnp.float32
    ).astype(jnp.bfloat16)
    incoming = lax.all_to_all(
        outgoing.reshape(GROUPS, SLOTS, share), GY, split_axis=0, concat_axis=0, tiled=True
    ).reshape(GROUPS * SLOTS, share)
    in_yl = swap(incoming, "yl")
    in_core = swap(incoming, "c")
    in_far = swap(in_yl, "c")
    order = jnp.stack(
        [yl * 2 + core, (1 - yl) * 2 + core, yl * 2 + 1 - core, (1 - yl) * 2 + 1 - core]
    ).astype(jnp.int32)
    o0, o1, o2, o3 = experts(
        order, (incoming, in_yl, in_core, in_far), w_gate[0], w_up[0], w_down[0]
    )
    passed = (
        o1.astype(jnp.float32) + swap(o3, "c").astype(jnp.float32)
    ).astype(jnp.bfloat16)
    near = o0.astype(jnp.float32) + swap(o2, "c").astype(jnp.float32)
    summed = (near + swap(passed, "yl").astype(jnp.float32)).astype(jnp.bfloat16)
    returned = lax.all_to_all(
        summed.reshape(GROUPS, SLOTS, share), GY, split_axis=0, concat_axis=0, tiled=True
    ).reshape(GROUPS * SLOTS, share)
    moe = jnp.dot(
        blend, returned.astype(jnp.float32), precision=lax.Precision.HIGHEST,
        preferred_element_type=jnp.float32,
    )
    output = (residual.astype(jnp.float32) + moe).astype(jnp.bfloat16)
    return (output, latent_cache)


def solution(mesh):
    fine = Mesh(mesh.devices.reshape(YL, CORES, YH, XS, ZS), GX + GY)
    return jax.shard_map(
        shards,
        mesh=fine,
        in_specs=(
            P(GY, GX),
            P(),
            P(GY, None),
            P(GY, None),
            P(),
            P(),
            P(),
            P(GY, GX),
            P(GY, GX),
            P(GY, GX),
            P(GX, GY),
            P(GY, None, GX),
            P(GY, None, GX),
            P(GY, GX, None),
            P(GX + GY),
        ),
        out_specs=(P(GY, GX), P(GX + GY, None, None)),
        check_vma=False,
    )
```

```python
import jax
import jax.numpy as jnp
from jax import lax
from jax.experimental import pallas as pl
from jax.experimental.pallas import tpu as pltpu
from jax.sharding import Mesh, PartitionSpec as P

NOPE = 128
ROPE = 64
VDIM = 128
RANK = 512
PAGE = 16
KEY = RANK + ROPE
WIDE = 640

GX = ("yl", "c")
GY = ("yh", "x", "z")
YL, CORES, YH, XS, ZS = 2, 2, 2, 4, 8
GROUPS = YH * XS * ZS
PARTS = YL * CORES
SLOTS = 16
CHUNKS = 2
SWAP = [(0, 1), (1, 0)]

eps = 1e-06
masked_score = -1e30


def norm_rows(values, gain):
    mean_sq = jnp.mean(values * values, axis=-1, keepdims=True)
    return values * lax.rsqrt(mean_sq + eps) * gain


def angle_table(positions, width):
    exponents = jnp.arange(width // 2, dtype=jnp.float32) * (2.0 / width)
    freqs = jnp.power(10000.0, -exponents)
    return positions.astype(jnp.float32)[:, None] * freqs[None, :]


def rotate(values, cosine, sine):
    half = values.shape[-1] // 2
    first = values[..., :half]
    second = values[..., half:]
    return jnp.concatenate(
        [first * cosine - second * sine, second * cosine + first * sine], axis=-1
    )


def shift(values, axis, size, step):
    return lax.ppermute(values, axis, [(i, (i + step) % size) for i in range(size)])


def swap(values, axis):
    return lax.ppermute(values, axis, SWAP)


def spread(values, axis, size):
    blocks = jnp.broadcast_to(values[None], (size,) + values.shape)
    return lax.all_to_all(blocks, axis, split_axis=0, concat_axis=0, tiled=True)


def attention_kernel(
    meta, q_ref, qlo_ref, qpos_ref, a_own, a_oth, b_own, b_oth, wuv_ref, wo_ref, out_ref,
    best, total, accum, heads,
):
    step = pl.program_id(0)
    kmin, kmax, core = meta[16], meta[17], meta[18]

    @pl.when(step == 0)
    def _():
        best[...] = jnp.full_like(best, masked_score)
        total[...] = jnp.zeros_like(total)
        accum[...] = jnp.zeros_like(accum)

    def block(base, colour, own_ref, oth_ref):
        @pl.when((base <= kmax) & (base + 1023 >= kmin))
        def _():
            queries = q_ref[...]
            lo, hi = qlo_ref[...], qpos_ref[...]
            row = lax.broadcasted_iota(jnp.int32, (1, 256), 1)
            place = base + (row // 32) * 128 + row % 32 + colour * 32
            scores, masks = [], []
            for ref, side in ((own_ref, core), (oth_ref, 1 - core)):
                keys = ref[0]
                raw = lax.dot_general(
                    queries, keys, (((1,), (1,)), ((), ())), preferred_element_type=jnp.float32
                )
                where = place + side * 64
                mask = (where >= lo) & (where <= hi)
                scores.append(jnp.where(mask, raw, masked_score))
                masks.append(mask)
            old = best[...]
            new = jnp.maximum(
                old,
                jnp.maximum(
                    jnp.max(scores[0], axis=-1, keepdims=True),
                    jnp.max(scores[1], axis=-1, keepdims=True),
                ),
            )
            alpha = jnp.exp(old - new)
            best[...] = new
            grown = total[...] * alpha
            fresh = accum[...] * alpha
            for ref, score, mask in ((own_ref, scores[0], masks[0]), (oth_ref, scores[1], masks[1])):
                weight = jnp.where(mask, jnp.exp(score - new), 0.0)
                grown = grown + jnp.sum(weight, axis=-1, keepdims=True)
                fresh = fresh + jnp.dot(
                    weight.astype(jnp.bfloat16), ref[0, :, :RANK],
                    preferred_element_type=jnp.float32,
                )
            total[...] = grown
            accum[...] = fresh

    block(meta[step], 0, a_own, a_oth)
    block(meta[8 + step], 1, b_own, b_oth)

    @pl.when(step == pl.num_programs(0) - 1)
    def _():
        rows = out_ref.shape[0]
        mixed = (accum[...] / total[...]).astype(jnp.bfloat16)
        for h in range(wuv_ref.shape[0]):
            heads[:, h * VDIM : (h + 1) * VDIM] = jnp.dot(
                mixed[h * rows : (h + 1) * rows], wuv_ref[h], preferred_element_type=jnp.float32
            ).astype(jnp.bfloat16)
        out_ref[...] = lax.dot_general(
            heads[...], wo_ref[...], (((1,), (1,)), ((), ())), preferred_element_type=jnp.float32
        )


def attention(meta, queries, qlo, qpos, keys, w_uv, w_o):
    head_rows = queries.shape[0]
    rows = head_rows // w_uv.shape[0]

    def whole(shape):
        return pl.BlockSpec(shape, lambda i, m: (0,) * len(shape))

    key_spec = pl.BlockSpec((1, 256, WIDE), lambda i, m: (i, 0, 0))
    return pl.pallas_call(
        attention_kernel,
        out_shape=jax.ShapeDtypeStruct((rows, w_o.shape[0]), jnp.float32),
        grid_spec=pltpu.PrefetchScalarGridSpec(
            num_scalar_prefetch=1,
            grid=(8,),
            in_specs=[
                whole(queries.shape), whole(qlo.shape), whole(qpos.shape),
                key_spec, key_spec, key_spec, key_spec,
                whole(w_uv.shape), whole(w_o.shape),
            ],
            out_specs=whole((rows, w_o.shape[0])),
            scratch_shapes=[
                pltpu.VMEM((head_rows, 1), jnp.float32),
                pltpu.VMEM((head_rows, 1), jnp.float32),
                pltpu.VMEM((head_rows, RANK), jnp.float32),
                pltpu.VMEM((rows, w_uv.shape[0] * VDIM), jnp.bfloat16),
            ],
        ),
        cost_estimate=pl.CostEstimate(
            flops=9_000_000_000, bytes_accessed=16_000_000, transcendentals=4_000_000
        ),
        compiler_params=pltpu.CompilerParams(
            dimension_semantics=("arbitrary",), vmem_limit_bytes=40 << 20
        ),
    )(meta, queries, qlo, qpos, *keys, w_uv, w_o)


def expert_kernel(order, x0, x1, x2, x3, wg_ref, wu_ref, wd_ref, o0, o1, o2, o3):
    share = x0.shape[1]
    gate = jnp.zeros((x0.shape[0], wg_ref.shape[0]), jnp.float32)
    across = (((1,), (1,)), ((), ()))
    upper = gate
    starts = [pl.multiple_of(order[j] * share, share) for j in range(4)]
    for start, ref in zip(starts, (x0, x1, x2, x3)):
        piece = ref[...]
        gate = gate + lax.dot_general(
            piece, wg_ref[:, pl.ds(start, share)], across, preferred_element_type=jnp.float32
        )
        upper = upper + lax.dot_general(
            piece, wu_ref[:, pl.ds(start, share)], across, preferred_element_type=jnp.float32
        )
    active = (gate / (1.0 + jnp.exp(-gate)) * upper).astype(jnp.bfloat16)
    for start, ref in zip(starts, (o0, o1, o2, o3)):
        ref[...] = jnp.dot(
            active, wd_ref[:, pl.ds(start, share)], preferred_element_type=jnp.float32
        ).astype(jnp.bfloat16)


def experts(order, pieces, w_gate, w_up, w_down):
    count, share = pieces[0].shape
    tile = 256

    def whole(shape):
        return pl.BlockSpec(shape, lambda i, m: (0,) * len(shape))

    row_spec = pl.BlockSpec((tile, share), lambda i, m: (i, 0))
    return pl.pallas_call(
        expert_kernel,
        out_shape=[jax.ShapeDtypeStruct((count, share), jnp.bfloat16)] * 4,
        grid_spec=pltpu.PrefetchScalarGridSpec(
            num_scalar_prefetch=1,
            grid=(count // tile,),
            in_specs=[row_spec] * 4
            + [whole(w_gate.shape), whole(w_up.shape), whole(w_down.shape)],
            out_specs=[row_spec] * 4,
        ),
        cost_estimate=pl.CostEstimate(
            flops=4_400_000_000, bytes_accessed=13_000_000, transcendentals=400_000
        ),
        compiler_params=pltpu.CompilerParams(
            dimension_semantics=("arbitrary",), vmem_limit_bytes=40 << 20
        ),
    )(order, *pieces, w_gate, w_up, w_down)


def shards(
    hidden, segment_ids, expert_ids, route_weight, attn_gain, kv_gain, ffn_gain,
    w_q, w_kv_a, w_kv_b, w_o, w_gate, w_up, w_down, page_table,
):
    row_count, share = hidden.shape
    yl, core = lax.axis_index("yl"), lax.axis_index("c")
    yh, x, z = (lax.axis_index(name) for name in GY)
    row_start = ((yh * XS + x) * ZS + z) * row_count
    head_count = w_q.shape[1] // (NOPE + ROPE)
    depth = w_q.shape[0]

    expand_rows = w_kv_b.shape[0]
    local_expand = (
        w_kv_b.reshape(expand_rows, head_count, NOPE + VDIM)
        .transpose(1, 0, 2)
        .reshape(expand_rows * head_count, NOPE + VDIM)
    )
    tail_cols = w_kv_a.shape[1] - 128
    packed = jnp.concatenate(
        [
            w_q, local_expand, w_o.T, w_kv_a,
            jnp.zeros((depth, 128 - tail_cols), jnp.bfloat16),
        ],
        axis=1,
    )
    late = packed.shape[1] - 256
    near_weights = spread(packed, "z", ZS).reshape(ZS * depth, packed.shape[1])
    weights = lax.all_gather(near_weights[:, :late], ("yh", "x"), axis=0, tiled=True)
    tail = near_weights[:, late + 128 : late + 128 + tail_cols]
    latent_packed = jnp.concatenate(
        [near_weights[:, late : late + 128], tail.reshape(ZS * depth * tail_cols // 128, 128)],
        axis=0,
    )
    latent_all = spread(latent_packed, ("yh", "x"), YH * XS)
    latent_main = latent_all[:, : ZS * depth].reshape(GROUPS * depth, 128)
    latent_tail = latent_all[:, ZS * depth :].reshape(GROUPS * depth, tail_cols)

    positions = row_start + jnp.arange(row_count, dtype=jnp.int32)
    own_segments = lax.dynamic_slice_in_dim(segment_ids, row_start, row_count)
    prompt_start = jnp.sum(
        (segment_ids[None, :] < own_segments[:, None]).astype(jnp.int32), axis=1
    )
    angles = angle_table(positions - prompt_start, ROPE)
    cosine, sine = jnp.cos(angles), jnp.sin(angles)

    full_rows = lax.all_gather(hidden, GX, axis=1, tiled=True)
    normed = norm_rows(full_rows.astype(jnp.float32), attn_gain).astype(jnp.bfloat16)

    kv_part = jnp.concatenate(
        [
            jnp.dot(normed, latent_main, preferred_element_type=jnp.float32),
            jnp.dot(normed, latent_tail, preferred_element_type=jnp.float32),
        ],
        axis=1,
    )
    kv_raw = lax.all_gather(kv_part, GX, axis=1, tiled=True)
    half = row_count // CORES
    kv_half = lax.dynamic_slice_in_dim(kv_raw, core * half, half)
    keys = jnp.concatenate(
        [
            norm_rows(kv_half[:, :RANK], kv_gain),
            rotate(
                kv_half[:, RANK:],
                lax.dynamic_slice_in_dim(cosine, core * half, half),
                lax.dynamic_slice_in_dim(sine, core * half, half),
            ),
            jnp.zeros((half, WIDE - KEY), jnp.float32),
        ],
        axis=1,
    ).astype(jnp.bfloat16)
    along_z = spread(keys, "z", ZS)
    quarter = half // 2
    a0 = along_z[:, :quarter].reshape(1, ZS * quarter, WIDE)
    b0 = along_z[:, quarter:].reshape(1, ZS * quarter, WIDE)
    b1 = jnp.concatenate([b0, swap(b0, "yh")], axis=0)
    a1 = jnp.concatenate([a0] + [shift(a0, "x", XS, k) for k in range(1, XS)], axis=0)
    a_own = jnp.concatenate([a1, swap(a1, "yh")], axis=0)
    b_own = jnp.concatenate([b1] + [shift(b1, "x", XS, k) for k in range(1, XS)], axis=0)
    a_oth, b_oth = swap(a_own, "c"), swap(b_own, "c")
    steps = jnp.arange(8, dtype=jnp.int32)
    base_a = ((yh ^ (steps // 4)) * XS + (x - steps % 4) % XS) * (ZS * row_count)
    base_b = ((yh ^ (steps % 2)) * XS + (x - steps // 2) % XS) * (ZS * row_count)
    meta = jnp.concatenate(
        [
            base_a, base_b,
            jnp.stack([prompt_start[0], row_start + row_count - 1, core]).astype(jnp.int32),
        ]
    ).astype(jnp.int32)

    pages = []
    for i in range(page_table.shape[0]):
        page = page_table[i]
        group, inside = page // (row_count // PAGE), page % (row_count // PAGE)
        far_yh, far_x = (group // (XS * ZS)) ^ yh, (x - (group // ZS) % XS) % XS
        start = (group % ZS) * quarter + (inside % 2) * PAGE
        is_own = inside // 4 == core
        index_a, index_b = far_yh * XS + far_x, far_x * YH + far_yh
        size = (1, PAGE, WIDE)
        from_a = jnp.where(
            is_own,
            lax.dynamic_slice(a_own, (index_a, start, 0), size),
            lax.dynamic_slice(a_oth, (index_a, start, 0), size),
        )
        from_b = jnp.where(
            is_own,
            lax.dynamic_slice(b_own, (index_b, start, 0), size),
            lax.dynamic_slice(b_oth, (index_b, start, 0), size),
        )
        pages.append(jnp.where((inside % 4) // 2 == 0, from_a, from_b))
    latent_cache = jnp.concatenate(pages, axis=0)[:, :, :KEY]

    q_cols = w_q.shape[1]
    expand = (
        weights[:, q_cols : q_cols + NOPE + VDIM]
        .reshape(GROUPS, head_count, expand_rows, NOPE + VDIM)
        .transpose(1, 0, 2, 3)
        .reshape(head_count, RANK, NOPE + VDIM)
    )
    out_rows = weights[:, q_cols + NOPE + VDIM :]
    scale = (NOPE + ROPE) ** (-0.5)
    query = jnp.dot(normed, weights[:, :q_cols], preferred_element_type=jnp.float32).reshape(
        row_count, head_count, NOPE + ROPE
    )
    q_nope = query[:, :, :NOPE].astype(jnp.bfloat16)
    absorbed = (
        jnp.einsum("thn,hrn->htr", q_nope, expand[:, :, :NOPE], preferred_element_type=jnp.float32)
        * scale
    ).astype(jnp.bfloat16)
    rotated = (
        rotate(query[:, :, NOPE:], cosine[:, None, :], sine[:, None, :]) * scale
    ).astype(jnp.bfloat16)
    blank = jnp.zeros((head_count, row_count, WIDE - KEY), jnp.bfloat16)
    queries = jnp.concatenate(
        [absorbed, jnp.transpose(rotated, (1, 0, 2)), blank], axis=2
    ).reshape(head_count * row_count, WIDE)
    qlo = jnp.tile(prompt_start.astype(jnp.int32), head_count)[:, None]
    qpos = jnp.tile(positions, head_count)[:, None]
    head_terms = attention(
        meta, queries, qlo, qpos, (a_own, a_oth, b_own, b_oth), expand[:, :, NOPE:], out_rows
    )

    term_blocks = head_terms.reshape(row_count, PARTS, share).transpose(1, 0, 2)
    head_sum = jnp.sum(
        lax.all_to_all(term_blocks, GX, split_axis=0, concat_axis=0, tiled=True), axis=0
    )
    residual = (hidden.astype(jnp.float32) + head_sum).astype(jnp.bfloat16)
    wide = residual.astype(jnp.float32)
    squares = lax.all_gather(jnp.sum(wide * wide, axis=1)[None], GX, axis=0, tiled=True)
    mean_sq = jnp.sum(squares, axis=0)[:, None] * (1.0 / (share * PARTS))
    own_gain = lax.dynamic_slice_in_dim(ffn_gain, (yl * CORES + core) * share, share)
    ffn_in = (wide * lax.rsqrt(mean_sq + eps) * own_gain).astype(jnp.bfloat16)

    top_count = expert_ids.shape[1]
    expert_range = jnp.arange(GROUPS, dtype=jnp.int32)
    chosen = (expert_ids[:, :, None] == expert_range).astype(jnp.float32)
    named = jnp.sum(chosen, axis=1)
    earlier = (
        jnp.arange(row_count)[:, None] > jnp.arange(row_count)[None, :]
    ).astype(jnp.float32)
    before = jnp.dot(earlier, named, preferred_element_type=jnp.float32)
    ranks = jnp.sum(chosen * before[:, None, :], axis=2).astype(jnp.int32)
    slots = expert_ids * SLOTS + ranks
    order = jnp.stack(
        [yl * 2 + core, (1 - yl) * 2 + core, yl * 2 + 1 - core, (1 - yl) * 2 + 1 - core]
    ).astype(jnp.int32)
    gate_t, up_t, down = w_gate[0].T, w_up[0].T, w_down[0]
    chunk = SLOTS // CHUNKS
    counter = jnp.arange(GROUPS * chunk, dtype=jnp.int32)
    moe = jnp.zeros((row_count, share), jnp.float32)
    for part in range(CHUNKS):
        slot_range = counter // chunk * SLOTS + counter % chunk + part * chunk
        pick = jnp.zeros((GROUPS * chunk, row_count), jnp.bool_)
        blend = jnp.zeros((row_count, GROUPS * chunk), jnp.float32)
        for k in range(top_count):
            pick = pick | (slot_range[:, None] == slots[:, k][None, :])
            blend = blend + jnp.where(
                slots[:, k][:, None] == slot_range[None, :], route_weight[:, k][:, None], 0.0
            )
        outgoing = jnp.dot(
            pick.astype(jnp.bfloat16), ffn_in, preferred_element_type=jnp.float32
        ).astype(jnp.bfloat16)
        incoming = lax.all_to_all(
            outgoing.reshape(GROUPS, chunk, share), GY, split_axis=0, concat_axis=0, tiled=True
        ).reshape(GROUPS * chunk, share)
        in_yl = swap(incoming, "yl")
        in_core = swap(incoming, "c")
        in_far = swap(in_yl, "c")
        o0, o1, o2, o3 = experts(order, (incoming, in_yl, in_core, in_far), gate_t, up_t, down)
        passed = (
            o1.astype(jnp.float32) + swap(o3, "c").astype(jnp.float32)
        ).astype(jnp.bfloat16)
        near = o0.astype(jnp.float32) + swap(o2, "c").astype(jnp.float32)
        summed = (near + swap(passed, "yl").astype(jnp.float32)).astype(jnp.bfloat16)
        returned = lax.all_to_all(
            summed.reshape(GROUPS, chunk, share), GY, split_axis=0, concat_axis=0, tiled=True
        ).reshape(GROUPS * chunk, share)
        moe = moe + jnp.dot(
            blend, returned.astype(jnp.float32), precision=lax.Precision.HIGHEST,
            preferred_element_type=jnp.float32,
        )
    output = (residual.astype(jnp.float32) + moe).astype(jnp.bfloat16)
    return (output, latent_cache)


def solution(mesh):
    fine = Mesh(mesh.devices.reshape(YL, CORES, YH, XS, ZS), GX + GY)
    return jax.shard_map(
        shards,
        mesh=fine,
        in_specs=(
            P(GY, GX),
            P(),
            P(GY, None),
            P(GY, None),
            P(),
            P(),
            P(),
            P(GY, GX),
            P(GY, GX),
            P(GY, GX),
            P(GX, GY),
            P(GY, None, GX),
            P(GY, None, GX),
            P(GY, GX, None),
            P(GX + GY),
        ),
        out_specs=(P(GY, GX), P(GX + GY, None, None)),
        check_vma=False,
    )
```

```python
import jax
import jax.numpy as jnp
from jax import lax
from jax.experimental import pallas as pl
from jax.experimental.pallas import tpu as pltpu
from jax.sharding import Mesh, PartitionSpec as P

NOPE = 128
ROPE = 64
VDIM = 128
RANK = 512
PAGE = 16
KEY = RANK + ROPE
WIDE = 640

GX = ("yl", "c")
GY = ("yh", "x", "z")
YL, CORES, YH, XS, ZS = 2, 2, 2, 4, 8
GROUPS = YH * XS * ZS
PARTS = YL * CORES
SLOTS = 16
CHUNKS = 2
SWAP = [(0, 1), (1, 0)]

eps = 1e-06
masked_score = -1e30


def norm_rows(values, gain):
    mean_sq = jnp.mean(values * values, axis=-1, keepdims=True)
    return values * lax.rsqrt(mean_sq + eps) * gain


def angle_table(positions, width):
    exponents = jnp.arange(width // 2, dtype=jnp.float32) * (2.0 / width)
    freqs = jnp.power(10000.0, -exponents)
    return positions.astype(jnp.float32)[:, None] * freqs[None, :]


def rotate(values, cosine, sine):
    half = values.shape[-1] // 2
    first = values[..., :half]
    second = values[..., half:]
    return jnp.concatenate(
        [first * cosine - second * sine, second * cosine + first * sine], axis=-1
    )


def shift(values, axis, size, step):
    return lax.ppermute(values, axis, [(i, (i + step) % size) for i in range(size)])


def swap(values, axis):
    return lax.ppermute(values, axis, SWAP)


def spread(values, axis, size):
    blocks = jnp.broadcast_to(values[None], (size,) + values.shape)
    return lax.all_to_all(blocks, axis, split_axis=0, concat_axis=0, tiled=True)


def attention_kernel(
    meta, q_ref, qlo_ref, qpos_ref, a_own, a_oth, b_own, b_oth, wuv_ref, wo_ref, out_ref,
    best, total, accum, heads,
):
    step = pl.program_id(0)
    kmin, kmax, core = meta[16], meta[17], meta[18]

    @pl.when(step == 0)
    def _():
        best[...] = jnp.full_like(best, masked_score)
        total[...] = jnp.zeros_like(total)
        accum[...] = jnp.zeros_like(accum)

    def block(base, colour, own_ref, oth_ref):
        @pl.when((base <= kmax) & (base + 1023 >= kmin))
        def _():
            queries = q_ref[...]
            lo, hi = qlo_ref[...], qpos_ref[...]
            row = lax.broadcasted_iota(jnp.int32, (1, 256), 1)
            place = base + (row // 32) * 128 + row % 32 + colour * 32
            scores, masks = [], []
            for ref, side in ((own_ref, core), (oth_ref, 1 - core)):
                keys = ref[0]
                raw = lax.dot_general(
                    queries, keys, (((1,), (1,)), ((), ())), preferred_element_type=jnp.float32
                )
                where = place + side * 64
                mask = (where >= lo) & (where <= hi)
                scores.append(jnp.where(mask, raw, masked_score))
                masks.append(mask)
            old = best[...]
            new = jnp.maximum(
                old,
                jnp.maximum(
                    jnp.max(scores[0], axis=-1, keepdims=True),
                    jnp.max(scores[1], axis=-1, keepdims=True),
                ),
            )
            alpha = jnp.exp(old - new)
            best[...] = new
            grown = total[...] * alpha
            fresh = accum[...] * alpha
            for ref, score, mask in ((own_ref, scores[0], masks[0]), (oth_ref, scores[1], masks[1])):
                weight = jnp.where(mask, jnp.exp(score - new), 0.0)
                grown = grown + jnp.sum(weight, axis=-1, keepdims=True)
                fresh = fresh + jnp.dot(
                    weight.astype(jnp.bfloat16), ref[0, :, :RANK],
                    preferred_element_type=jnp.float32,
                )
            total[...] = grown
            accum[...] = fresh

    block(meta[step], 0, a_own, a_oth)
    block(meta[8 + step], 1, b_own, b_oth)

    @pl.when(step == pl.num_programs(0) - 1)
    def _():
        rows = out_ref.shape[0]
        mixed = (accum[...] / total[...]).astype(jnp.bfloat16)
        for h in range(wuv_ref.shape[0]):
            heads[:, h * VDIM : (h + 1) * VDIM] = jnp.dot(
                mixed[h * rows : (h + 1) * rows], wuv_ref[h], preferred_element_type=jnp.float32
            ).astype(jnp.bfloat16)
        out_ref[...] = lax.dot_general(
            heads[...], wo_ref[...], (((1,), (1,)), ((), ())), preferred_element_type=jnp.float32
        )


def attention(meta, queries, qlo, qpos, keys, w_uv, w_o):
    head_rows = queries.shape[0]
    rows = head_rows // w_uv.shape[0]

    def whole(shape):
        return pl.BlockSpec(shape, lambda i, m: (0,) * len(shape))

    key_spec = pl.BlockSpec((1, 256, WIDE), lambda i, m: (i, 0, 0))
    return pl.pallas_call(
        attention_kernel,
        out_shape=jax.ShapeDtypeStruct((rows, w_o.shape[0]), jnp.float32),
        grid_spec=pltpu.PrefetchScalarGridSpec(
            num_scalar_prefetch=1,
            grid=(8,),
            in_specs=[
                whole(queries.shape), whole(qlo.shape), whole(qpos.shape),
                key_spec, key_spec, key_spec, key_spec,
                whole(w_uv.shape), whole(w_o.shape),
            ],
            out_specs=whole((rows, w_o.shape[0])),
            scratch_shapes=[
                pltpu.VMEM((head_rows, 1), jnp.float32),
                pltpu.VMEM((head_rows, 1), jnp.float32),
                pltpu.VMEM((head_rows, RANK), jnp.float32),
                pltpu.VMEM((rows, w_uv.shape[0] * VDIM), jnp.bfloat16),
            ],
        ),
        cost_estimate=pl.CostEstimate(
            flops=9_000_000_000, bytes_accessed=16_000_000, transcendentals=4_000_000
        ),
        compiler_params=pltpu.CompilerParams(
            dimension_semantics=("arbitrary",), vmem_limit_bytes=40 << 20
        ),
    )(meta, queries, qlo, qpos, *keys, w_uv, w_o)


def expert_kernel(order, x0, x1, x2, x3, wg_ref, wu_ref, wd_ref, o0, o1, o2, o3):
    share = x0.shape[1]
    gate = jnp.zeros((x0.shape[0], wg_ref.shape[0]), jnp.float32)
    across = (((1,), (1,)), ((), ()))
    upper = gate
    starts = [pl.multiple_of(order[j] * share, share) for j in range(4)]
    for start, ref in zip(starts, (x0, x1, x2, x3)):
        piece = ref[...]
        gate = gate + lax.dot_general(
            piece, wg_ref[:, pl.ds(start, share)], across, preferred_element_type=jnp.float32
        )
        upper = upper + lax.dot_general(
            piece, wu_ref[:, pl.ds(start, share)], across, preferred_element_type=jnp.float32
        )
    active = (gate / (1.0 + jnp.exp(-gate)) * upper).astype(jnp.bfloat16)
    for start, ref in zip(starts, (o0, o1, o2, o3)):
        ref[...] = jnp.dot(
            active, wd_ref[:, pl.ds(start, share)], preferred_element_type=jnp.float32
        ).astype(jnp.bfloat16)


def experts(order, pieces, w_gate, w_up, w_down):
    count, share = pieces[0].shape
    tile = 256

    def whole(shape):
        return pl.BlockSpec(shape, lambda i, m: (0,) * len(shape))

    row_spec = pl.BlockSpec((tile, share), lambda i, m: (i, 0))
    return pl.pallas_call(
        expert_kernel,
        out_shape=[jax.ShapeDtypeStruct((count, share), jnp.bfloat16)] * 4,
        grid_spec=pltpu.PrefetchScalarGridSpec(
            num_scalar_prefetch=1,
            grid=(count // tile,),
            in_specs=[row_spec] * 4
            + [whole(w_gate.shape), whole(w_up.shape), whole(w_down.shape)],
            out_specs=[row_spec] * 4,
        ),
        cost_estimate=pl.CostEstimate(
            flops=4_400_000_000, bytes_accessed=13_000_000, transcendentals=400_000
        ),
        compiler_params=pltpu.CompilerParams(
            dimension_semantics=("arbitrary",), vmem_limit_bytes=40 << 20
        ),
    )(order, *pieces, w_gate, w_up, w_down)


def shards(
    hidden, segment_ids, expert_ids, route_weight, attn_gain, kv_gain, ffn_gain,
    w_q, w_kv_a, w_kv_b, w_o, w_gate, w_up, w_down, page_table,
):
    row_count, share = hidden.shape
    yl, core = lax.axis_index("yl"), lax.axis_index("c")
    yh, x, z = (lax.axis_index(name) for name in GY)
    row_start = ((yh * XS + x) * ZS + z) * row_count
    head_count = w_q.shape[1] // (NOPE + ROPE)
    depth = w_q.shape[0]

    expand_rows = w_kv_b.shape[0]
    local_expand = (
        w_kv_b.reshape(expand_rows, head_count, NOPE + VDIM)
        .transpose(1, 0, 2)
        .reshape(expand_rows * head_count, NOPE + VDIM)
    )
    tail_cols = w_kv_a.shape[1] - 128
    packed = jnp.concatenate(
        [
            w_q, local_expand, w_o.T, w_kv_a,
            jnp.zeros((depth, 128 - tail_cols), jnp.bfloat16),
        ],
        axis=1,
    )
    late = packed.shape[1] - 256
    crowd = YH * XS
    near_weights = spread(packed, ("yh", "x"), crowd).reshape(crowd * depth, packed.shape[1])
    weights = (
        lax.all_gather(near_weights[:, :late], "z", axis=0, tiled=True)
        .reshape(ZS, crowd, depth, late)
        .transpose(1, 0, 2, 3)
        .reshape(GROUPS * depth, late)
    )
    tail = near_weights[:, late + 128 : late + 128 + tail_cols]
    latent_packed = jnp.concatenate(
        [near_weights[:, late : late + 128], tail.reshape(crowd * depth * tail_cols // 128, 128)],
        axis=0,
    )
    latent_all = spread(latent_packed, "z", ZS)
    latent_main = (
        latent_all[:, : crowd * depth]
        .reshape(ZS, crowd, depth, 128)
        .transpose(1, 0, 2, 3)
        .reshape(GROUPS * depth, 128)
    )
    latent_tail = (
        latent_all[:, crowd * depth :]
        .reshape(ZS, crowd, depth * tail_cols // 128, 128)
        .transpose(1, 0, 2, 3)
        .reshape(GROUPS * depth, tail_cols)
    )

    positions = row_start + jnp.arange(row_count, dtype=jnp.int32)
    own_segments = lax.dynamic_slice_in_dim(segment_ids, row_start, row_count)
    prompt_start = jnp.sum(
        (segment_ids[None, :] < own_segments[:, None]).astype(jnp.int32), axis=1
    )
    angles = angle_table(positions - prompt_start, ROPE)
    cosine, sine = jnp.cos(angles), jnp.sin(angles)

    full_rows = lax.all_gather(hidden, GX, axis=1, tiled=True)
    normed = norm_rows(full_rows.astype(jnp.float32), attn_gain).astype(jnp.bfloat16)

    kv_part = jnp.concatenate(
        [
            jnp.dot(normed, latent_main, preferred_element_type=jnp.float32),
            jnp.dot(normed, latent_tail, preferred_element_type=jnp.float32),
        ],
        axis=1,
    )
    kv_raw = lax.all_gather(kv_part, GX, axis=1, tiled=True)
    half = row_count // CORES
    kv_half = lax.dynamic_slice_in_dim(kv_raw, core * half, half)
    keys = jnp.concatenate(
        [
            norm_rows(kv_half[:, :RANK], kv_gain),
            rotate(
                kv_half[:, RANK:],
                lax.dynamic_slice_in_dim(cosine, core * half, half),
                lax.dynamic_slice_in_dim(sine, core * half, half),
            ),
            jnp.zeros((half, WIDE - KEY), jnp.float32),
        ],
        axis=1,
    ).astype(jnp.bfloat16)
    along_z = spread(keys, "z", ZS)
    quarter = half // 2
    a0 = along_z[:, :quarter].reshape(1, ZS * quarter, WIDE)
    b0 = along_z[:, quarter:].reshape(1, ZS * quarter, WIDE)
    b1 = jnp.concatenate([b0, swap(b0, "yh")], axis=0)
    a1 = jnp.concatenate([a0] + [shift(a0, "x", XS, k) for k in range(1, XS)], axis=0)
    a_own = jnp.concatenate([a1, swap(a1, "yh")], axis=0)
    b_own = jnp.concatenate([b1] + [shift(b1, "x", XS, k) for k in range(1, XS)], axis=0)
    a_oth, b_oth = swap(a_own, "c"), swap(b_own, "c")
    steps = jnp.arange(8, dtype=jnp.int32)
    base_a = ((yh ^ (steps // 4)) * XS + (x - steps % 4) % XS) * (ZS * row_count)
    base_b = ((yh ^ (steps % 2)) * XS + (x - steps // 2) % XS) * (ZS * row_count)
    meta = jnp.concatenate(
        [
            base_a, base_b,
            jnp.stack([prompt_start[0], row_start + row_count - 1, core]).astype(jnp.int32),
        ]
    ).astype(jnp.int32)

    pages = []
    for i in range(page_table.shape[0]):
        page = page_table[i]
        group, inside = page // (row_count // PAGE), page % (row_count // PAGE)
        far_yh, far_x = (group // (XS * ZS)) ^ yh, (x - (group // ZS) % XS) % XS
        start = (group % ZS) * quarter + (inside % 2) * PAGE
        is_own = inside // 4 == core
        index_a, index_b = far_yh * XS + far_x, far_x * YH + far_yh
        size = (1, PAGE, WIDE)
        from_a = jnp.where(
            is_own,
            lax.dynamic_slice(a_own, (index_a, start, 0), size),
            lax.dynamic_slice(a_oth, (index_a, start, 0), size),
        )
        from_b = jnp.where(
            is_own,
            lax.dynamic_slice(b_own, (index_b, start, 0), size),
            lax.dynamic_slice(b_oth, (index_b, start, 0), size),
        )
        pages.append(jnp.where((inside % 4) // 2 == 0, from_a, from_b))
    latent_cache = jnp.concatenate(pages, axis=0)[:, :, :KEY]

    q_cols = w_q.shape[1]
    expand = (
        weights[:, q_cols : q_cols + NOPE + VDIM]
        .reshape(GROUPS, head_count, expand_rows, NOPE + VDIM)
        .transpose(1, 0, 2, 3)
        .reshape(head_count, RANK, NOPE + VDIM)
    )
    out_rows = weights[:, q_cols + NOPE + VDIM :]
    scale = (NOPE + ROPE) ** (-0.5)
    query = jnp.dot(normed, weights[:, :q_cols], preferred_element_type=jnp.float32).reshape(
        row_count, head_count, NOPE + ROPE
    )
    q_nope = query[:, :, :NOPE].astype(jnp.bfloat16)
    absorbed = (
        jnp.einsum("thn,hrn->htr", q_nope, expand[:, :, :NOPE], preferred_element_type=jnp.float32)
        * scale
    ).astype(jnp.bfloat16)
    rotated = (
        rotate(query[:, :, NOPE:], cosine[:, None, :], sine[:, None, :]) * scale
    ).astype(jnp.bfloat16)
    blank = jnp.zeros((head_count, row_count, WIDE - KEY), jnp.bfloat16)
    queries = jnp.concatenate(
        [absorbed, jnp.transpose(rotated, (1, 0, 2)), blank], axis=2
    ).reshape(head_count * row_count, WIDE)
    qlo = jnp.tile(prompt_start.astype(jnp.int32), head_count)[:, None]
    qpos = jnp.tile(positions, head_count)[:, None]
    head_terms = attention(
        meta, queries, qlo, qpos, (a_own, a_oth, b_own, b_oth), expand[:, :, NOPE:], out_rows
    )

    term_blocks = head_terms.reshape(row_count, PARTS, share).transpose(1, 0, 2)
    head_sum = jnp.sum(
        lax.all_to_all(term_blocks, GX, split_axis=0, concat_axis=0, tiled=True), axis=0
    )
    residual = (hidden.astype(jnp.float32) + head_sum).astype(jnp.bfloat16)
    wide = residual.astype(jnp.float32)
    squares = lax.all_gather(jnp.sum(wide * wide, axis=1)[None], GX, axis=0, tiled=True)
    mean_sq = jnp.sum(squares, axis=0)[:, None] * (1.0 / (share * PARTS))
    own_gain = lax.dynamic_slice_in_dim(ffn_gain, (yl * CORES + core) * share, share)
    ffn_in = (wide * lax.rsqrt(mean_sq + eps) * own_gain).astype(jnp.bfloat16)

    top_count = expert_ids.shape[1]
    expert_range = jnp.arange(GROUPS, dtype=jnp.int32)
    chosen = (expert_ids[:, :, None] == expert_range).astype(jnp.float32)
    named = jnp.sum(chosen, axis=1)
    earlier = (
        jnp.arange(row_count)[:, None] > jnp.arange(row_count)[None, :]
    ).astype(jnp.float32)
    before = jnp.dot(earlier, named, preferred_element_type=jnp.float32)
    ranks = jnp.sum(chosen * before[:, None, :], axis=2).astype(jnp.int32)
    slots = expert_ids * SLOTS + ranks
    order = jnp.stack(
        [yl * 2 + core, (1 - yl) * 2 + core, yl * 2 + 1 - core, (1 - yl) * 2 + 1 - core]
    ).astype(jnp.int32)
    gate_t, up_t, down = w_gate[0].T, w_up[0].T, w_down[0]
    chunk = SLOTS // CHUNKS
    counter = jnp.arange(GROUPS * chunk, dtype=jnp.int32)
    moe = jnp.zeros((row_count, share), jnp.float32)
    for part in range(CHUNKS):
        slot_range = counter // chunk * SLOTS + counter % chunk + part * chunk
        pick = jnp.zeros((GROUPS * chunk, row_count), jnp.bool_)
        blend = jnp.zeros((row_count, GROUPS * chunk), jnp.float32)
        for k in range(top_count):
            pick = pick | (slot_range[:, None] == slots[:, k][None, :])
            blend = blend + jnp.where(
                slots[:, k][:, None] == slot_range[None, :], route_weight[:, k][:, None], 0.0
            )
        outgoing = jnp.dot(
            pick.astype(jnp.bfloat16), ffn_in, preferred_element_type=jnp.float32
        ).astype(jnp.bfloat16)
        incoming = lax.all_to_all(
            outgoing.reshape(GROUPS, chunk, share), GY, split_axis=0, concat_axis=0, tiled=True
        ).reshape(GROUPS * chunk, share)
        in_yl = swap(incoming, "yl")
        in_core = swap(incoming, "c")
        in_far = swap(in_yl, "c")
        o0, o1, o2, o3 = experts(order, (incoming, in_yl, in_core, in_far), gate_t, up_t, down)
        passed = (
            o1.astype(jnp.float32) + swap(o3, "c").astype(jnp.float32)
        ).astype(jnp.bfloat16)
        near = o0.astype(jnp.float32) + swap(o2, "c").astype(jnp.float32)
        summed = (near + swap(passed, "yl").astype(jnp.float32)).astype(jnp.bfloat16)
        returned = lax.all_to_all(
            summed.reshape(GROUPS, chunk, share), GY, split_axis=0, concat_axis=0, tiled=True
        ).reshape(GROUPS * chunk, share)
        moe = moe + jnp.dot(
            blend, returned.astype(jnp.float32), precision=lax.Precision.HIGHEST,
            preferred_element_type=jnp.float32,
        )
    output = (residual.astype(jnp.float32) + moe).astype(jnp.bfloat16)
    return (output, latent_cache)


def solution(mesh):
    fine = Mesh(mesh.devices.reshape(YL, CORES, YH, XS, ZS), GX + GY)
    return jax.shard_map(
        shards,
        mesh=fine,
        in_specs=(
            P(GY, GX),
            P(),
            P(GY, None),
            P(GY, None),
            P(),
            P(),
            P(),
            P(GY, GX),
            P(GY, GX),
            P(GY, GX),
            P(GX, GY),
            P(GY, None, GX),
            P(GY, None, GX),
            P(GY, GX, None),
            P(GX + GY),
        ),
        out_specs=(P(GY, GX), P(GX + GY, None, None)),
        check_vma=False,
    )
```

```python
import jax
import jax.numpy as jnp
from jax import lax
from jax.experimental import pallas as pl
from jax.experimental.pallas import tpu as pltpu
from jax.sharding import Mesh, PartitionSpec as P


NOPE = 128
ROPE = 64
VDIM = 128
RANK = 512
PAGE = 16
KEY = RANK + ROPE
WIDE = 640

GX = ("yl", "c")
GY = ("yh", "x", "z")
YL, CORES, YH, XS, ZS = 2, 2, 2, 4, 8
GROUPS = YH * XS * ZS
PARTS = YL * CORES
SLOTS = 16
CHUNKS = 2
SWAP = [(0, 1), (1, 0)]

eps = 1e-06
masked_score = -1e30


def norm_rows(values, gain):
    mean_sq = jnp.mean(values * values, axis=-1, keepdims=True)
    return values * lax.rsqrt(mean_sq + eps) * gain


def angle_table(positions, width):
    exponents = jnp.arange(width // 2, dtype=jnp.float32) * (2.0 / width)
    freqs = jnp.power(10000.0, -exponents)
    return positions.astype(jnp.float32)[:, None] * freqs[None, :]


def rotate(values, cosine, sine):
    half = values.shape[-1] // 2
    first = values[..., :half]
    second = values[..., half:]
    return jnp.concatenate(
        [first * cosine - second * sine, second * cosine + first * sine], axis=-1
    )


def shift(values, axis, size, step):
    return lax.ppermute(values, axis, [(i, (i + step) % size) for i in range(size)])


def swap(values, axis):
    return lax.ppermute(values, axis, SWAP)


def spread(values, axis, size):
    blocks = jnp.broadcast_to(values[None], (size,) + values.shape)
    return lax.all_to_all(blocks, axis, split_axis=0, concat_axis=0, tiled=True)


def attention_kernel(
    meta, q_ref, qlo_ref, qpos_ref, a_own, a_oth, b_own, b_oth, wuv_ref, wo_ref, out_ref,
    best, total, accum, heads,
):
    step = pl.program_id(0)
    kmin, kmax, core = meta[16], meta[17], meta[18]

    @pl.when(step == 0)
    def _():
        best[...] = jnp.full_like(best, masked_score)
        total[...] = jnp.zeros_like(total)
        accum[...] = jnp.zeros_like(accum)

    def block(base, colour, own_ref, oth_ref):
        @pl.when((base <= kmax) & (base + 1023 >= kmin))
        def _():
            queries = q_ref[...]
            lo, hi = qlo_ref[...], qpos_ref[...]
            row = lax.broadcasted_iota(jnp.int32, (1, 256), 1)
            place = base + (row // 32) * 128 + row % 32 + colour * 32
            scores, masks = [], []
            for ref, side in ((own_ref, core), (oth_ref, 1 - core)):
                keys = ref[0]
                raw = lax.dot_general(
                    queries, keys, (((1,), (1,)), ((), ())), preferred_element_type=jnp.float32
                )
                where = place + side * 64
                mask = (where >= lo) & (where <= hi)
                scores.append(jnp.where(mask, raw, masked_score))
                masks.append(mask)
            old = best[...]
            new = jnp.maximum(
                old,
                jnp.maximum(
                    jnp.max(scores[0], axis=-1, keepdims=True),
                    jnp.max(scores[1], axis=-1, keepdims=True),
                ),
            )
            alpha = jnp.exp(old - new)
            best[...] = new
            grown = total[...] * alpha
            fresh = accum[...] * alpha
            for ref, score, mask in ((own_ref, scores[0], masks[0]), (oth_ref, scores[1], masks[1])):
                weight = jnp.where(mask, jnp.exp(score - new), 0.0)
                grown = grown + jnp.sum(weight, axis=-1, keepdims=True)
                fresh = fresh + jnp.dot(
                    weight.astype(jnp.bfloat16), ref[0, :, :RANK],
                    preferred_element_type=jnp.float32,
                )
            total[...] = grown
            accum[...] = fresh

    block(meta[step], 0, a_own, a_oth)
    block(meta[8 + step], 1, b_own, b_oth)

    @pl.when(step == pl.num_programs(0) - 1)
    def _():
        rows = out_ref.shape[2]
        mixed = (accum[...] / total[...]).astype(jnp.bfloat16)
        for h in range(wuv_ref.shape[0]):
            heads[:, h * VDIM : (h + 1) * VDIM] = jnp.dot(
                mixed[h * rows : (h + 1) * rows], wuv_ref[h], preferred_element_type=jnp.float32
            ).astype(jnp.bfloat16)
        for part in range(PARTS):
            wo_rows = wo_ref.shape[0] // PARTS
            out_ref[part // CORES, part % CORES] = lax.dot_general(
                heads[...], wo_ref[part * wo_rows : (part + 1) * wo_rows],
                (((1,), (1,)), ((), ())), preferred_element_type=jnp.float32,
            )


def attention(meta, queries, qlo, qpos, keys, w_uv, w_o):
    head_rows = queries.shape[0]
    rows = head_rows // w_uv.shape[0]
    out_dims = (YL, CORES, rows, w_o.shape[0] // PARTS)

    def whole(shape):
        return pl.BlockSpec(shape, lambda i, m: (0,) * len(shape))

    key_spec = pl.BlockSpec((1, 256, WIDE), lambda i, m: (i, 0, 0))
    return pl.pallas_call(
        attention_kernel,
        out_shape=jax.ShapeDtypeStruct(out_dims, jnp.float32),
        grid_spec=pltpu.PrefetchScalarGridSpec(
            num_scalar_prefetch=1,
            grid=(8,),
            in_specs=[
                whole(queries.shape), whole(qlo.shape), whole(qpos.shape),
                key_spec, key_spec, key_spec, key_spec,
                whole(w_uv.shape), whole(w_o.shape),
            ],
            out_specs=whole(out_dims),
            scratch_shapes=[
                pltpu.VMEM((head_rows, 1), jnp.float32),
                pltpu.VMEM((head_rows, 1), jnp.float32),
                pltpu.VMEM((head_rows, RANK), jnp.float32),
                pltpu.VMEM((rows, w_uv.shape[0] * VDIM), jnp.bfloat16),
            ],
        ),
        cost_estimate=pl.CostEstimate(
            flops=9_000_000_000, bytes_accessed=16_000_000, transcendentals=4_000_000
        ),
        compiler_params=pltpu.CompilerParams(
            dimension_semantics=("arbitrary",), vmem_limit_bytes=40 << 20
        ),
    )(meta, queries, qlo, qpos, *keys, w_uv, w_o)


def expert_kernel(order, x0, x1, x2, x3, wg_ref, wu_ref, wd_ref, o0, o1, o2, o3):
    share = x0.shape[1]
    gate = jnp.zeros((x0.shape[0], wg_ref.shape[0]), jnp.float32)
    across = (((1,), (1,)), ((), ()))
    upper = gate
    starts = [pl.multiple_of(order[j] * share, share) for j in range(4)]
    for start, ref in zip(starts, (x0, x1, x2, x3)):
        piece = ref[...]
        gate = gate + lax.dot_general(
            piece, wg_ref[:, pl.ds(start, share)], across, preferred_element_type=jnp.float32
        )
        upper = upper + lax.dot_general(
            piece, wu_ref[:, pl.ds(start, share)], across, preferred_element_type=jnp.float32
        )
    active = (gate / (1.0 + jnp.exp(-gate)) * upper).astype(jnp.bfloat16)
    for start, ref in zip(starts, (o0, o1, o2, o3)):
        ref[...] = jnp.dot(
            active, wd_ref[:, pl.ds(start, share)], preferred_element_type=jnp.float32
        ).astype(jnp.bfloat16)


def experts(order, pieces, w_gate, w_up, w_down):
    count, share = pieces[0].shape
    tile = 256

    def whole(shape):
        return pl.BlockSpec(shape, lambda i, m: (0,) * len(shape))

    row_spec = pl.BlockSpec((tile, share), lambda i, m: (i, 0))
    return pl.pallas_call(
        expert_kernel,
        out_shape=[jax.ShapeDtypeStruct((count, share), jnp.bfloat16)] * 4,
        grid_spec=pltpu.PrefetchScalarGridSpec(
            num_scalar_prefetch=1,
            grid=(count // tile,),
            in_specs=[row_spec] * 4
            + [whole(w_gate.shape), whole(w_up.shape), whole(w_down.shape)],
            out_specs=[row_spec] * 4,
        ),
        cost_estimate=pl.CostEstimate(
            flops=4_400_000_000, bytes_accessed=13_000_000, transcendentals=400_000
        ),
        compiler_params=pltpu.CompilerParams(
            dimension_semantics=("arbitrary",), vmem_limit_bytes=40 << 20
        ),
    )(order, *pieces, w_gate, w_up, w_down)


def layer(
    hidden, segment_ids, expert_ids, route_weight, attn_gain, kv_gain, ffn_gain,
    w_q, w_kv_a, w_kv_b, w_o, w_gate, w_up, w_down, page_table,
):
    row_count, share = hidden.shape
    yl, core = lax.axis_index("yl"), lax.axis_index("c")
    yh, x, z = (lax.axis_index(name) for name in GY)
    row_start = ((yh * XS + x) * ZS + z) * row_count
    head_count = w_q.shape[1] // (NOPE + ROPE)
    depth = w_q.shape[0]

    expand_rows = w_kv_b.shape[0]
    local_expand = (
        w_kv_b.reshape(expand_rows, head_count, NOPE + VDIM)
        .transpose(1, 0, 2)
        .reshape(expand_rows * head_count, NOPE + VDIM)
    )
    packed = jnp.concatenate([w_q, local_expand, w_o.T], axis=1)
    crowd, late = YH * XS, packed.shape[1]
    tail_cols = w_kv_a.shape[1] - 128
    latent_packed = jnp.concatenate(
        [w_kv_a[:, :128], w_kv_a[:, 128:].reshape(depth * tail_cols // 128, 128)], axis=0
    )
    latent_all = spread(latent_packed, GY, GROUPS)
    latent_main = latent_all[:, :depth].reshape(GROUPS * depth, 128)
    latent_tail = latent_all[:, depth:].reshape(GROUPS * depth, tail_cols)
    w1, w2, w3 = (shift(packed[None], "x", XS, k) for k in range(1, XS))
    circle = jnp.concatenate([w3, w2, w1, packed[None], w3, w2, w1], axis=0)
    along_x = lax.dynamic_slice_in_dim(circle, XS - 1 - x, XS)
    across_yh = swap(along_x, "yh")
    near_weights = jnp.where(
        yh == 0,
        jnp.concatenate([along_x, across_yh], axis=0),
        jnp.concatenate([across_yh, along_x], axis=0),
    )
    weights = (
        lax.all_gather(near_weights.reshape(crowd * depth, late), "z", axis=0, tiled=True)
        .reshape(ZS, crowd, depth, late)
        .transpose(1, 0, 2, 3)
        .reshape(GROUPS * depth, late)
    )

    positions = row_start + jnp.arange(row_count, dtype=jnp.int32)
    own_segments = lax.dynamic_slice_in_dim(segment_ids, row_start, row_count)
    prompt_start = jnp.sum(
        (segment_ids[None, :] < own_segments[:, None]).astype(jnp.int32), axis=1
    )
    angles = angle_table(positions - prompt_start, ROPE)
    cosine, sine = jnp.cos(angles), jnp.sin(angles)

    full_rows = lax.all_gather(hidden, GX, axis=1, tiled=True)
    normed = norm_rows(full_rows.astype(jnp.float32), attn_gain).astype(jnp.bfloat16)

    kv_part = jnp.concatenate(
        [
            jnp.dot(normed, latent_main, preferred_element_type=jnp.float32),
            jnp.dot(normed, latent_tail, preferred_element_type=jnp.float32),
        ],
        axis=1,
    )
    kv_raw = lax.all_gather(kv_part, GX, axis=1, tiled=True)
    half = row_count // CORES
    kv_half = lax.dynamic_slice_in_dim(kv_raw, core * half, half)
    keys = jnp.concatenate(
        [
            norm_rows(kv_half[:, :RANK], kv_gain),
            rotate(
                kv_half[:, RANK:],
                lax.dynamic_slice_in_dim(cosine, core * half, half),
                lax.dynamic_slice_in_dim(sine, core * half, half),
            ),
            jnp.zeros((half, WIDE - KEY), jnp.float32),
        ],
        axis=1,
    ).astype(jnp.bfloat16)
    along_z = spread(keys, "z", ZS)
    quarter = half // 2
    a0 = along_z[:, :quarter].reshape(1, ZS * quarter, WIDE)
    b0 = along_z[:, quarter:].reshape(1, ZS * quarter, WIDE)
    b1 = jnp.concatenate([b0, swap(b0, "yh")], axis=0)
    a1 = jnp.concatenate([a0] + [shift(a0, "x", XS, k) for k in range(1, XS)], axis=0)
    a_own = jnp.concatenate([a1, swap(a1, "yh")], axis=0)
    b_own = jnp.concatenate([b1] + [shift(b1, "x", XS, k) for k in range(1, XS)], axis=0)
    a_oth, b_oth = swap(a_own, "c"), swap(b_own, "c")
    steps = jnp.arange(8, dtype=jnp.int32)
    base_a = ((yh ^ (steps // 4)) * XS + (x - steps % 4) % XS) * (ZS * row_count)
    base_b = ((yh ^ (steps % 2)) * XS + (x - steps // 2) % XS) * (ZS * row_count)
    meta = jnp.concatenate(
        [
            base_a, base_b,
            jnp.stack([prompt_start[0], row_start + row_count - 1, core]).astype(jnp.int32),
        ]
    ).astype(jnp.int32)

    pages = []
    for i in range(page_table.shape[0]):
        page = page_table[i]
        group, inside = page // (row_count // PAGE), page % (row_count // PAGE)
        far_yh, far_x = (group // (XS * ZS)) ^ yh, (x - (group // ZS) % XS) % XS
        start = (group % ZS) * quarter + (inside % 2) * PAGE
        is_own = inside // 4 == core
        index_a, index_b = far_yh * XS + far_x, far_x * YH + far_yh
        size = (1, PAGE, WIDE)
        from_a = jnp.where(
            is_own,
            lax.dynamic_slice(a_own, (index_a, start, 0), size),
            lax.dynamic_slice(a_oth, (index_a, start, 0), size),
        )
        from_b = jnp.where(
            is_own,
            lax.dynamic_slice(b_own, (index_b, start, 0), size),
            lax.dynamic_slice(b_oth, (index_b, start, 0), size),
        )
        pages.append(jnp.where((inside % 4) // 2 == 0, from_a, from_b))
    latent_cache = jnp.concatenate(pages, axis=0)[:, :, :KEY]

    q_cols = w_q.shape[1]
    expand = (
        weights[:, q_cols : q_cols + NOPE + VDIM]
        .reshape(GROUPS, head_count, expand_rows, NOPE + VDIM)
        .transpose(1, 0, 2, 3)
        .reshape(head_count, RANK, NOPE + VDIM)
    )
    out_rows = weights[:, q_cols + NOPE + VDIM :]
    scale = (NOPE + ROPE) ** (-0.5)
    query = jnp.dot(normed, weights[:, :q_cols], preferred_element_type=jnp.float32).reshape(
        row_count, head_count, NOPE + ROPE
    )
    q_nope = query[:, :, :NOPE].astype(jnp.bfloat16)
    absorbed = (
        jnp.einsum("thn,hrn->htr", q_nope, expand[:, :, :NOPE], preferred_element_type=jnp.float32)
        * scale
    ).astype(jnp.bfloat16)
    rotated = (
        rotate(query[:, :, NOPE:], cosine[:, None, :], sine[:, None, :]) * scale
    ).astype(jnp.bfloat16)
    blank = jnp.zeros((head_count, row_count, WIDE - KEY), jnp.bfloat16)
    queries = jnp.concatenate(
        [absorbed, jnp.transpose(rotated, (1, 0, 2)), blank], axis=2
    ).reshape(head_count * row_count, WIDE)
    qlo = jnp.tile(prompt_start.astype(jnp.int32), head_count)[:, None]
    qpos = jnp.tile(positions, head_count)[:, None]
    head_terms = attention(
        meta, queries, qlo, qpos, (a_own, a_oth, b_own, b_oth), expand[:, :, NOPE:], out_rows
    )

    kept = lax.dynamic_index_in_dim(head_terms, core, 1, keepdims=False)
    given = lax.dynamic_index_in_dim(head_terms, 1 - core, 1, keepdims=False)
    pair_sum = kept + swap(given, "c")
    mine = lax.dynamic_index_in_dim(pair_sum, yl, 0, keepdims=False)
    theirs = lax.dynamic_index_in_dim(pair_sum, 1 - yl, 0, keepdims=False)
    head_sum = mine + swap(theirs, "yl")
    residual = (hidden.astype(jnp.float32) + head_sum).astype(jnp.bfloat16)
    wide = residual.astype(jnp.float32)
    squares = lax.all_gather(jnp.sum(wide * wide, axis=1)[None], GX, axis=0, tiled=True)
    mean_sq = jnp.sum(squares, axis=0)[:, None] * (1.0 / (share * PARTS))
    own_gain = lax.dynamic_slice_in_dim(ffn_gain, (yl * CORES + core) * share, share)
    ffn_in = (wide * lax.rsqrt(mean_sq + eps) * own_gain).astype(jnp.bfloat16)

    top_count = expert_ids.shape[1]
    expert_range = jnp.arange(GROUPS, dtype=jnp.int32)
    chosen = (expert_ids[:, :, None] == expert_range).astype(jnp.float32)
    named = jnp.sum(chosen, axis=1)
    earlier = (
        jnp.arange(row_count)[:, None] > jnp.arange(row_count)[None, :]
    ).astype(jnp.float32)
    before = jnp.dot(earlier, named, preferred_element_type=jnp.float32)
    ranks = jnp.sum(chosen * before[:, None, :], axis=2).astype(jnp.int32)
    slots = expert_ids * SLOTS + ranks
    order = jnp.stack(
        [yl * 2 + core, (1 - yl) * 2 + core, yl * 2 + 1 - core, (1 - yl) * 2 + 1 - core]
    ).astype(jnp.int32)
    gate_t, up_t, down = w_gate[0].T, w_up[0].T, w_down[0]
    chunk = SLOTS // CHUNKS
    counter = jnp.arange(GROUPS * chunk, dtype=jnp.int32)
    moe = jnp.zeros((row_count, share), jnp.float32)
    for part in range(CHUNKS):
        slot_range = counter // chunk * SLOTS + counter % chunk + part * chunk
        pick = jnp.zeros((GROUPS * chunk, row_count), jnp.bool_)
        blend = jnp.zeros((row_count, GROUPS * chunk), jnp.float32)
        for k in range(top_count):
            pick = pick | (slot_range[:, None] == slots[:, k][None, :])
            blend = blend + jnp.where(
                slots[:, k][:, None] == slot_range[None, :], route_weight[:, k][:, None], 0.0
            )
        outgoing = jnp.dot(
            pick.astype(jnp.bfloat16), ffn_in, preferred_element_type=jnp.float32
        ).astype(jnp.bfloat16)
        incoming = lax.all_to_all(
            outgoing.reshape(GROUPS, chunk, share), GY, split_axis=0, concat_axis=0, tiled=True
        ).reshape(GROUPS * chunk, share)
        in_yl = swap(incoming, "yl")
        in_core = swap(incoming, "c")
        in_far = swap(in_yl, "c")
        o0, o1, o2, o3 = experts(order, (incoming, in_yl, in_core, in_far), gate_t, up_t, down)
        passed = (
            o1.astype(jnp.float32) + swap(o3, "c").astype(jnp.float32)
        ).astype(jnp.bfloat16)
        near = o0.astype(jnp.float32) + swap(o2, "c").astype(jnp.float32)
        summed = (near + swap(passed, "yl").astype(jnp.float32)).astype(jnp.bfloat16)
        returned = lax.all_to_all(
            summed.reshape(GROUPS, chunk, share), GY, split_axis=0, concat_axis=0, tiled=True
        ).reshape(GROUPS * chunk, share)
        moe = moe + jnp.dot(
            blend, returned.astype(jnp.float32), precision=lax.Precision.HIGHEST,
            preferred_element_type=jnp.float32,
        )
    output = (residual.astype(jnp.float32) + moe).astype(jnp.bfloat16)
    return (output, latent_cache)


def solution(mesh):
    fine = Mesh(mesh.devices.reshape(YL, CORES, YH, XS, ZS), GX + GY)
    return jax.shard_map(
        layer,
        mesh=fine,
        in_specs=(
            P(GY, GX),
            P(),
            P(GY, None),
            P(GY, None),
            P(),
            P(),
            P(),
            P(GY, GX),
            P(GY, GX),
            P(GY, GX),
            P(GX, GY),
            P(GY, None, GX),
            P(GY, None, GX),
            P(GY, GX, None),
            P(GX + GY),
        ),
        out_specs=(P(GY, GX), P(GX + GY, None, None)),
        check_vma=False,
    )
```

```python
import jax
import jax.numpy as jnp
from jax import lax
from jax.experimental import pallas as pl
from jax.experimental.pallas import tpu as pltpu
from jax.sharding import Mesh, PartitionSpec as P


NOPE = 128
ROPE = 64
VDIM = 128
RANK = 512
PAGE = 16
KEY = RANK + ROPE
WIDE = 640

GX = ("yl", "c")
GY = ("yh", "x", "z")
YL, CORES, YH, XS, ZS = 2, 2, 2, 4, 8
GROUPS = YH * XS * ZS
PARTS = YL * CORES
SLOTS = 16
CHUNKS = 2
SWAP = [(0, 1), (1, 0)]

eps = 1e-06
masked_score = -1e30


def norm_rows(values, gain):
    mean_sq = jnp.mean(values * values, axis=-1, keepdims=True)
    return values * lax.rsqrt(mean_sq + eps) * gain


def angle_table(positions, width):
    exponents = jnp.arange(width // 2, dtype=jnp.float32) * (2.0 / width)
    freqs = jnp.power(10000.0, -exponents)
    return positions.astype(jnp.float32)[:, None] * freqs[None, :]


def rotate(values, cosine, sine):
    half = values.shape[-1] // 2
    first = values[..., :half]
    second = values[..., half:]
    return jnp.concatenate(
        [first * cosine - second * sine, second * cosine + first * sine], axis=-1
    )


def shift(values, axis, size, step):
    return lax.ppermute(values, axis, [(i, (i + step) % size) for i in range(size)])


def swap(values, axis):
    return lax.ppermute(values, axis, SWAP)


def spread(values, axis, size):
    blocks = jnp.broadcast_to(values[None], (size,) + values.shape)
    return lax.all_to_all(blocks, axis, split_axis=0, concat_axis=0, tiled=True)


def attention_kernel(
    meta, q_ref, qlo_ref, qpos_ref, a_own, a_oth, b_own, b_oth, wuv_ref, out_ref,
    best, total, accum,
):
    step = pl.program_id(0)
    kmin, kmax, core = meta[16], meta[17], meta[18]

    @pl.when(step == 0)
    def _():
        best[...] = jnp.full_like(best, masked_score)
        total[...] = jnp.zeros_like(total)
        accum[...] = jnp.zeros_like(accum)

    def block(base, colour, own_ref, oth_ref):
        @pl.when((base <= kmax) & (base + 1023 >= kmin))
        def _():
            queries = q_ref[...]
            lo, hi = qlo_ref[...], qpos_ref[...]
            row = lax.broadcasted_iota(jnp.int32, (1, 256), 1)
            place = base + (row // 32) * 128 + row % 32 + colour * 32
            scores, masks = [], []
            for ref, side in ((own_ref, core), (oth_ref, 1 - core)):
                keys = ref[0]
                raw = lax.dot_general(
                    queries, keys, (((1,), (1,)), ((), ())), preferred_element_type=jnp.float32
                )
                where = place + side * 64
                mask = (where >= lo) & (where <= hi)
                scores.append(jnp.where(mask, raw, masked_score))
                masks.append(mask)
            old = best[...]
            new = jnp.maximum(
                old,
                jnp.maximum(
                    jnp.max(scores[0], axis=-1, keepdims=True),
                    jnp.max(scores[1], axis=-1, keepdims=True),
                ),
            )
            alpha = jnp.exp(old - new)
            best[...] = new
            grown = total[...] * alpha
            fresh = accum[...] * alpha
            for ref, score, mask in ((own_ref, scores[0], masks[0]), (oth_ref, scores[1], masks[1])):
                weight = jnp.where(mask, jnp.exp(score - new), 0.0)
                grown = grown + jnp.sum(weight, axis=-1, keepdims=True)
                fresh = fresh + jnp.dot(
                    weight.astype(jnp.bfloat16), ref[0, :, :RANK],
                    preferred_element_type=jnp.float32,
                )
            total[...] = grown
            accum[...] = fresh

    block(meta[step], 0, a_own, a_oth)
    block(meta[8 + step], 1, b_own, b_oth)

    @pl.when(step == pl.num_programs(0) - 1)
    def _():
        rows = out_ref.shape[0]
        mixed = (accum[...] / total[...]).astype(jnp.bfloat16)
        for h in range(wuv_ref.shape[0]):
            out_ref[:, h * VDIM : (h + 1) * VDIM] = jnp.dot(
                mixed[h * rows : (h + 1) * rows], wuv_ref[h], preferred_element_type=jnp.float32
            ).astype(jnp.bfloat16)


def project_kernel(heads_ref, wo_ref, out_ref):
    heads = heads_ref[...]
    crowds = wo_ref.shape[1] // PARTS
    for part in range(PARTS):
        rows = jnp.concatenate(
            [
                wo_ref[z, part * crowds + j]
                for j in range(crowds)
                for z in range(wo_ref.shape[0])
            ],
            axis=0,
        )
        out_ref[part // CORES, part % CORES] = lax.dot_general(
            heads, rows, (((1,), (1,)), ((), ())), preferred_element_type=jnp.float32
        )


def project(heads_out, out_rows):
    zs, crowd, depth, _ = out_rows.shape
    width = zs * crowd * depth // PARTS
    return pl.pallas_call(
        project_kernel,
        out_shape=jax.ShapeDtypeStruct(
            (YL, CORES, heads_out.shape[0], width), jnp.float32
        ),
        in_specs=[pl.BlockSpec(memory_space=pltpu.VMEM)] * 2,
        out_specs=pl.BlockSpec(memory_space=pltpu.VMEM),
        cost_estimate=pl.CostEstimate(
            flops=270_000_000, bytes_accessed=3_000_000, transcendentals=0
        ),
        compiler_params=pltpu.CompilerParams(vmem_limit_bytes=24 << 20),
    )(heads_out, out_rows)


def attention(meta, queries, qlo, qpos, keys, w_uv):
    head_rows = queries.shape[0]
    rows = head_rows // w_uv.shape[0]
    out_dims = (rows, w_uv.shape[0] * VDIM)

    def whole(shape):
        return pl.BlockSpec(shape, lambda i, m: (0,) * len(shape))

    key_spec = pl.BlockSpec((1, 256, WIDE), lambda i, m: (i, 0, 0))
    return pl.pallas_call(
        attention_kernel,
        out_shape=jax.ShapeDtypeStruct(out_dims, jnp.bfloat16),
        grid_spec=pltpu.PrefetchScalarGridSpec(
            num_scalar_prefetch=1,
            grid=(8,),
            in_specs=[
                whole(queries.shape), whole(qlo.shape), whole(qpos.shape),
                key_spec, key_spec, key_spec, key_spec,
                whole(w_uv.shape),
            ],
            out_specs=whole(out_dims),
            scratch_shapes=[
                pltpu.VMEM((head_rows, 1), jnp.float32),
                pltpu.VMEM((head_rows, 1), jnp.float32),
                pltpu.VMEM((head_rows, RANK), jnp.float32),
            ],
        ),
        cost_estimate=pl.CostEstimate(
            flops=9_000_000_000, bytes_accessed=16_000_000, transcendentals=4_000_000
        ),
        compiler_params=pltpu.CompilerParams(
            dimension_semantics=("arbitrary",), vmem_limit_bytes=40 << 20
        ),
    )(meta, queries, qlo, qpos, *keys, w_uv)


def expert_kernel(order, x0, x1, x2, x3, wg_ref, wu_ref, wd_ref, o0, o1, o2, o3):
    share = x0.shape[1]
    gate = jnp.zeros((x0.shape[0], wg_ref.shape[0]), jnp.float32)
    across = (((1,), (1,)), ((), ()))
    upper = gate
    starts = [pl.multiple_of(order[j] * share, share) for j in range(4)]
    for start, ref in zip(starts, (x0, x1, x2, x3)):
        piece = ref[...]
        gate = gate + lax.dot_general(
            piece, wg_ref[:, pl.ds(start, share)], across, preferred_element_type=jnp.float32
        )
        upper = upper + lax.dot_general(
            piece, wu_ref[:, pl.ds(start, share)], across, preferred_element_type=jnp.float32
        )
    active = (gate / (1.0 + jnp.exp(-gate)) * upper).astype(jnp.bfloat16)
    for start, ref in zip(starts, (o0, o1, o2, o3)):
        ref[...] = jnp.dot(
            active, wd_ref[:, pl.ds(start, share)], preferred_element_type=jnp.float32
        ).astype(jnp.bfloat16)


def experts(order, pieces, w_gate, w_up, w_down):
    count, share = pieces[0].shape
    tile = 256

    def whole(shape):
        return pl.BlockSpec(shape, lambda i, m: (0,) * len(shape))

    row_spec = pl.BlockSpec((tile, share), lambda i, m: (i, 0))
    return pl.pallas_call(
        expert_kernel,
        out_shape=[jax.ShapeDtypeStruct((count, share), jnp.bfloat16)] * 4,
        grid_spec=pltpu.PrefetchScalarGridSpec(
            num_scalar_prefetch=1,
            grid=(count // tile,),
            in_specs=[row_spec] * 4
            + [whole(w_gate.shape), whole(w_up.shape), whole(w_down.shape)],
            out_specs=[row_spec] * 4,
        ),
        cost_estimate=pl.CostEstimate(
            flops=4_400_000_000, bytes_accessed=13_000_000, transcendentals=400_000
        ),
        compiler_params=pltpu.CompilerParams(
            dimension_semantics=("arbitrary",), vmem_limit_bytes=40 << 20
        ),
    )(order, *pieces, w_gate, w_up, w_down)


def layer(
    hidden, segment_ids, expert_ids, route_weight, attn_gain, kv_gain, ffn_gain,
    w_q, w_kv_a, w_kv_b, w_o, w_gate, w_up, w_down, page_table,
):
    row_count, share = hidden.shape
    yl, core = lax.axis_index("yl"), lax.axis_index("c")
    yh, x, z = (lax.axis_index(name) for name in GY)
    row_start = ((yh * XS + x) * ZS + z) * row_count
    head_count = w_q.shape[1] // (NOPE + ROPE)
    depth = w_q.shape[0]

    expand_rows = w_kv_b.shape[0]
    local_expand = (
        w_kv_b.reshape(expand_rows, head_count, NOPE + VDIM)
        .transpose(1, 0, 2)
        .reshape(expand_rows * head_count, NOPE + VDIM)
    )
    packed = jnp.concatenate([w_q, local_expand, w_o.T], axis=1)
    crowd, late = YH * XS, packed.shape[1]
    tail_cols = w_kv_a.shape[1] - 128
    latent_packed = jnp.concatenate(
        [w_kv_a[:, :128], w_kv_a[:, 128:].reshape(depth * tail_cols // 128, 128)], axis=0
    )
    latent_all = spread(latent_packed, GY, GROUPS)
    latent_main = latent_all[:, :depth].reshape(GROUPS * depth, 128)
    latent_tail = latent_all[:, depth:].reshape(GROUPS * depth, tail_cols)
    w1, w2, w3 = (shift(packed[None], "x", XS, k) for k in range(1, XS))
    circle = jnp.concatenate([w3, w2, w1, packed[None], w3, w2, w1], axis=0)
    along_x = lax.dynamic_slice_in_dim(circle, XS - 1 - x, XS)
    across_yh = swap(along_x, "yh")
    near_weights = jnp.where(
        yh == 0,
        jnp.concatenate([along_x, across_yh], axis=0),
        jnp.concatenate([across_yh, along_x], axis=0),
    )
    positions = row_start + jnp.arange(row_count, dtype=jnp.int32)
    own_segments = lax.dynamic_slice_in_dim(segment_ids, row_start, row_count)
    prompt_start = jnp.sum(
        (segment_ids[None, :] < own_segments[:, None]).astype(jnp.int32), axis=1
    )
    angles = angle_table(positions - prompt_start, ROPE)
    cosine, sine = jnp.cos(angles), jnp.sin(angles)

    full_rows = lax.all_gather(hidden, GX, axis=1, tiled=True)
    normed = norm_rows(full_rows.astype(jnp.float32), attn_gain).astype(jnp.bfloat16)

    kv_part = jnp.concatenate(
        [
            jnp.dot(normed, latent_main, preferred_element_type=jnp.float32),
            jnp.dot(normed, latent_tail, preferred_element_type=jnp.float32),
        ],
        axis=1,
    )
    kv_raw = lax.all_gather(kv_part, GX, axis=1, tiled=True)
    half = row_count // CORES
    kv_half = lax.dynamic_slice_in_dim(kv_raw, core * half, half)
    keys = jnp.concatenate(
        [
            norm_rows(kv_half[:, :RANK], kv_gain),
            rotate(
                kv_half[:, RANK:],
                lax.dynamic_slice_in_dim(cosine, core * half, half),
                lax.dynamic_slice_in_dim(sine, core * half, half),
            ),
            jnp.zeros((half, WIDE - KEY), jnp.float32),
        ],
        axis=1,
    ).astype(jnp.bfloat16)
    along_z = spread(keys, "z", ZS)
    near_weights = near_weights + along_z[0, 0, 0] * 0
    front_cols = w_q.shape[1] + NOPE + VDIM
    weights = (
        lax.all_gather(
            near_weights[:, :, :front_cols].reshape(crowd * depth, front_cols), "z",
            axis=0, tiled=True,
        )
        .reshape(ZS, crowd, depth, front_cols)
        .transpose(1, 0, 2, 3)
        .reshape(GROUPS * depth, front_cols)
    )
    out_rows = lax.all_gather(
        near_weights[:, :, front_cols:].reshape(crowd * depth, late - front_cols), "z",
        axis=0, tiled=True,
    ).reshape(ZS, crowd, depth, late - front_cols)
    quarter = half // 2
    a0 = along_z[:, :quarter].reshape(1, ZS * quarter, WIDE)
    b0 = along_z[:, quarter:].reshape(1, ZS * quarter, WIDE)
    b1 = jnp.concatenate([b0, swap(b0, "yh")], axis=0)
    a1 = jnp.concatenate([a0] + [shift(a0, "x", XS, k) for k in range(1, XS)], axis=0)
    a_own = jnp.concatenate([a1, swap(a1, "yh")], axis=0)
    b_own = jnp.concatenate([b1] + [shift(b1, "x", XS, k) for k in range(1, XS)], axis=0)
    a_oth, b_oth = swap(a_own, "c"), swap(b_own, "c")
    steps = jnp.arange(8, dtype=jnp.int32)
    base_a = ((yh ^ (steps // 4)) * XS + (x - steps % 4) % XS) * (ZS * row_count)
    base_b = ((yh ^ (steps % 2)) * XS + (x - steps // 2) % XS) * (ZS * row_count)
    meta = jnp.concatenate(
        [
            base_a, base_b,
            jnp.stack([prompt_start[0], row_start + row_count - 1, core]).astype(jnp.int32),
        ]
    ).astype(jnp.int32)

    pages = []
    for i in range(page_table.shape[0]):
        page = page_table[i]
        group, inside = page // (row_count // PAGE), page % (row_count // PAGE)
        far_yh, far_x = (group // (XS * ZS)) ^ yh, (x - (group // ZS) % XS) % XS
        start = (group % ZS) * quarter + (inside % 2) * PAGE
        is_own = inside // 4 == core
        index_a, index_b = far_yh * XS + far_x, far_x * YH + far_yh
        size = (1, PAGE, WIDE)
        from_a = jnp.where(
            is_own,
            lax.dynamic_slice(a_own, (index_a, start, 0), size),
            lax.dynamic_slice(a_oth, (index_a, start, 0), size),
        )
        from_b = jnp.where(
            is_own,
            lax.dynamic_slice(b_own, (index_b, start, 0), size),
            lax.dynamic_slice(b_oth, (index_b, start, 0), size),
        )
        pages.append(jnp.where((inside % 4) // 2 == 0, from_a, from_b))
    latent_cache = jnp.concatenate(pages, axis=0)[:, :, :KEY]

    q_cols = w_q.shape[1]
    expand = (
        weights[:, q_cols : q_cols + NOPE + VDIM]
        .reshape(GROUPS, head_count, expand_rows, NOPE + VDIM)
        .transpose(1, 0, 2, 3)
        .reshape(head_count, RANK, NOPE + VDIM)
    )
    scale = (NOPE + ROPE) ** (-0.5)
    query = jnp.dot(normed, weights[:, :q_cols], preferred_element_type=jnp.float32).reshape(
        row_count, head_count, NOPE + ROPE
    )
    q_nope = query[:, :, :NOPE].astype(jnp.bfloat16)
    absorbed = (
        jnp.einsum("thn,hrn->htr", q_nope, expand[:, :, :NOPE], preferred_element_type=jnp.float32)
        * scale
    ).astype(jnp.bfloat16)
    rotated = (
        rotate(query[:, :, NOPE:], cosine[:, None, :], sine[:, None, :]) * scale
    ).astype(jnp.bfloat16)
    blank = jnp.zeros((head_count, row_count, WIDE - KEY), jnp.bfloat16)
    queries = jnp.concatenate(
        [absorbed, jnp.transpose(rotated, (1, 0, 2)), blank], axis=2
    ).reshape(head_count * row_count, WIDE)
    qlo = jnp.tile(prompt_start.astype(jnp.int32), head_count)[:, None]
    qpos = jnp.tile(positions, head_count)[:, None]
    heads_out = attention(
        meta, queries, qlo, qpos, (a_own, a_oth, b_own, b_oth), expand[:, :, NOPE:]
    )
    head_terms = project(heads_out, out_rows)

    kept = lax.dynamic_index_in_dim(head_terms, core, 1, keepdims=False)
    given = lax.dynamic_index_in_dim(head_terms, 1 - core, 1, keepdims=False)
    pair_sum = kept + swap(given, "c")
    mine = lax.dynamic_index_in_dim(pair_sum, yl, 0, keepdims=False)
    theirs = lax.dynamic_index_in_dim(pair_sum, 1 - yl, 0, keepdims=False)
    head_sum = mine + swap(theirs, "yl")
    residual = (hidden.astype(jnp.float32) + head_sum).astype(jnp.bfloat16)
    wide = residual.astype(jnp.float32)
    squares = lax.all_gather(jnp.sum(wide * wide, axis=1)[None], GX, axis=0, tiled=True)
    mean_sq = jnp.sum(squares, axis=0)[:, None] * (1.0 / (share * PARTS))
    own_gain = lax.dynamic_slice_in_dim(ffn_gain, (yl * CORES + core) * share, share)
    ffn_in = (wide * lax.rsqrt(mean_sq + eps) * own_gain).astype(jnp.bfloat16)

    top_count = expert_ids.shape[1]
    expert_range = jnp.arange(GROUPS, dtype=jnp.int32)
    chosen = (expert_ids[:, :, None] == expert_range).astype(jnp.float32)
    named = jnp.sum(chosen, axis=1)
    earlier = (
        jnp.arange(row_count)[:, None] > jnp.arange(row_count)[None, :]
    ).astype(jnp.float32)
    before = jnp.dot(earlier, named, preferred_element_type=jnp.float32)
    ranks = jnp.sum(chosen * before[:, None, :], axis=2).astype(jnp.int32)
    slots = expert_ids * SLOTS + ranks
    order = jnp.stack(
        [yl * 2 + core, (1 - yl) * 2 + core, yl * 2 + 1 - core, (1 - yl) * 2 + 1 - core]
    ).astype(jnp.int32)
    gate_t, up_t, down = w_gate[0].T, w_up[0].T, w_down[0]
    chunk = SLOTS // CHUNKS
    counter = jnp.arange(GROUPS * chunk, dtype=jnp.int32)
    moe = jnp.zeros((row_count, share), jnp.float32)
    for part in range(CHUNKS):
        slot_range = counter // chunk * SLOTS + counter % chunk + part * chunk
        pick = jnp.zeros((GROUPS * chunk, row_count), jnp.bool_)
        blend = jnp.zeros((row_count, GROUPS * chunk), jnp.float32)
        for k in range(top_count):
            pick = pick | (slot_range[:, None] == slots[:, k][None, :])
            blend = blend + jnp.where(
                slots[:, k][:, None] == slot_range[None, :], route_weight[:, k][:, None], 0.0
            )
        outgoing = jnp.dot(
            pick.astype(jnp.bfloat16), ffn_in, preferred_element_type=jnp.float32
        ).astype(jnp.bfloat16)
        incoming = lax.all_to_all(
            outgoing.reshape(GROUPS, chunk, share), GY, split_axis=0, concat_axis=0, tiled=True
        ).reshape(GROUPS * chunk, share)
        in_yl = swap(incoming, "yl")
        in_core = swap(incoming, "c")
        in_far = swap(in_yl, "c")
        o0, o1, o2, o3 = experts(order, (incoming, in_yl, in_core, in_far), gate_t, up_t, down)
        passed = (
            o1.astype(jnp.float32) + swap(o3, "c").astype(jnp.float32)
        ).astype(jnp.bfloat16)
        near = o0.astype(jnp.float32) + swap(o2, "c").astype(jnp.float32)
        summed = (near + swap(passed, "yl").astype(jnp.float32)).astype(jnp.bfloat16)
        returned = lax.all_to_all(
            summed.reshape(GROUPS, chunk, share), GY, split_axis=0, concat_axis=0, tiled=True
        ).reshape(GROUPS * chunk, share)
        moe = moe + jnp.dot(
            blend, returned.astype(jnp.float32), precision=lax.Precision.HIGHEST,
            preferred_element_type=jnp.float32,
        )
    output = (residual.astype(jnp.float32) + moe).astype(jnp.bfloat16)
    return (output, latent_cache)


def solution(mesh):
    fine = Mesh(mesh.devices.reshape(YL, CORES, YH, XS, ZS), GX + GY)
    return jax.shard_map(
        layer,
        mesh=fine,
        in_specs=(
            P(GY, GX),
            P(),
            P(GY, None),
            P(GY, None),
            P(),
            P(),
            P(),
            P(GY, GX),
            P(GY, GX),
            P(GY, GX),
            P(GX, GY),
            P(GY, None, GX),
            P(GY, None, GX),
            P(GY, GX, None),
            P(GX + GY),
        ),
        out_specs=(P(GY, GX), P(GX + GY, None, None)),
        check_vma=False,
    )
```

```python
import jax
import jax.numpy as jnp
from jax import lax
from jax.experimental import pallas as pl
from jax.experimental.pallas import tpu as pltpu
from jax.sharding import Mesh, PartitionSpec as P


NOPE = 128
ROPE = 64
VDIM = 128
RANK = 512
PAGE = 16
KEY = RANK + ROPE
WIDE = 640

GX = ("yl", "c")
GY = ("yh", "x", "z")
YL, CORES, YH, XS, ZS = 2, 2, 2, 4, 8
GROUPS = YH * XS * ZS
PARTS = YL * CORES
SLOTS = 16
SWAP = [(0, 1), (1, 0)]

eps = 1e-06
masked_score = -1e30


def norm_rows(values, gain):
    mean_sq = jnp.mean(values * values, axis=-1, keepdims=True)
    return values * lax.rsqrt(mean_sq + eps) * gain


def angle_table(positions, width):
    exponents = jnp.arange(width // 2, dtype=jnp.float32) * (2.0 / width)
    freqs = jnp.power(10000.0, -exponents)
    return positions.astype(jnp.float32)[:, None] * freqs[None, :]


def rotate(values, cosine, sine):
    half = values.shape[-1] // 2
    first = values[..., :half]
    second = values[..., half:]
    return jnp.concatenate(
        [first * cosine - second * sine, second * cosine + first * sine], axis=-1
    )


def shift(values, axis, size, step):
    return lax.ppermute(values, axis, [(i, (i + step) % size) for i in range(size)])


def swap(values, axis):
    return lax.ppermute(values, axis, SWAP)


def spread(values, axis, size):
    blocks = jnp.broadcast_to(values[None], (size,) + values.shape)
    return lax.all_to_all(blocks, axis, split_axis=0, concat_axis=0, tiled=True)


def attention_kernel(
    meta, q_ref, qlo_ref, qpos_ref, a_own, a_oth, b_own, b_oth, wuv_ref, out_ref,
    best, total, accum,
):
    step = pl.program_id(0)
    kmin, kmax, core = meta[16], meta[17], meta[18]

    @pl.when(step == 0)
    def _():
        best[...] = jnp.full_like(best, masked_score)
        total[...] = jnp.zeros_like(total)
        accum[...] = jnp.zeros_like(accum)

    def block(base, colour, own_ref, oth_ref):
        @pl.when((base <= kmax) & (base + 1023 >= kmin))
        def _():
            queries = q_ref[...]
            lo, hi = qlo_ref[...], qpos_ref[...]
            row = lax.broadcasted_iota(jnp.int32, (1, 256), 1)
            place = base + (row // 32) * 128 + row % 32 + colour * 32
            scores, masks = [], []
            for ref, side in ((own_ref, core), (oth_ref, 1 - core)):
                keys = ref[0]
                raw = lax.dot_general(
                    queries, keys, (((1,), (1,)), ((), ())), preferred_element_type=jnp.float32
                )
                where = place + side * 64
                mask = (where >= lo) & (where <= hi)
                scores.append(jnp.where(mask, raw, masked_score))
                masks.append(mask)
            old = best[...]
            new = jnp.maximum(
                old,
                jnp.maximum(
                    jnp.max(scores[0], axis=-1, keepdims=True),
                    jnp.max(scores[1], axis=-1, keepdims=True),
                ),
            )
            alpha = jnp.exp(old - new)
            best[...] = new
            grown = total[...] * alpha
            fresh = accum[...] * alpha
            for ref, score, mask in ((own_ref, scores[0], masks[0]), (oth_ref, scores[1], masks[1])):
                weight = jnp.where(mask, jnp.exp(score - new), 0.0)
                grown = grown + jnp.sum(weight, axis=-1, keepdims=True)
                fresh = fresh + jnp.dot(
                    weight.astype(jnp.bfloat16), ref[0, :, :RANK],
                    preferred_element_type=jnp.float32,
                )
            total[...] = grown
            accum[...] = fresh

    block(meta[step], 0, a_own, a_oth)
    block(meta[8 + step], 1, b_own, b_oth)

    @pl.when(step == pl.num_programs(0) - 1)
    def _():
        rows = out_ref.shape[0]
        mixed = (accum[...] / total[...]).astype(jnp.bfloat16)
        for h in range(wuv_ref.shape[0]):
            out_ref[:, h * VDIM : (h + 1) * VDIM] = jnp.dot(
                mixed[h * rows : (h + 1) * rows], wuv_ref[h], preferred_element_type=jnp.float32
            ).astype(jnp.bfloat16)


def project_kernel(heads_ref, wo_ref, out_ref):
    heads = heads_ref[...]
    crowds = wo_ref.shape[1] // PARTS
    for part in range(PARTS):
        rows = jnp.concatenate(
            [
                wo_ref[z, part * crowds + j]
                for j in range(crowds)
                for z in range(wo_ref.shape[0])
            ],
            axis=0,
        )
        out_ref[part // CORES, part % CORES] = lax.dot_general(
            heads, rows, (((1,), (1,)), ((), ())), preferred_element_type=jnp.float32
        )


def project(heads_out, out_rows):
    zs, crowd, depth, _ = out_rows.shape
    width = zs * crowd * depth // PARTS
    return pl.pallas_call(
        project_kernel,
        out_shape=jax.ShapeDtypeStruct(
            (YL, CORES, heads_out.shape[0], width), jnp.float32
        ),
        in_specs=[pl.BlockSpec(memory_space=pltpu.VMEM)] * 2,
        out_specs=pl.BlockSpec(memory_space=pltpu.VMEM),
        cost_estimate=pl.CostEstimate(
            flops=270_000_000, bytes_accessed=3_000_000, transcendentals=0
        ),
        compiler_params=pltpu.CompilerParams(vmem_limit_bytes=24 << 20),
    )(heads_out, out_rows)


def attention(meta, queries, qlo, qpos, keys, w_uv):
    head_rows = queries.shape[0]
    rows = head_rows // w_uv.shape[0]
    out_dims = (rows, w_uv.shape[0] * VDIM)

    def whole(shape):
        return pl.BlockSpec(shape, lambda i, m: (0,) * len(shape))

    key_spec = pl.BlockSpec((1, 256, WIDE), lambda i, m: (i, 0, 0))
    return pl.pallas_call(
        attention_kernel,
        out_shape=jax.ShapeDtypeStruct(out_dims, jnp.bfloat16),
        grid_spec=pltpu.PrefetchScalarGridSpec(
            num_scalar_prefetch=1,
            grid=(8,),
            in_specs=[
                whole(queries.shape), whole(qlo.shape), whole(qpos.shape),
                key_spec, key_spec, key_spec, key_spec,
                whole(w_uv.shape),
            ],
            out_specs=whole(out_dims),
            scratch_shapes=[
                pltpu.VMEM((head_rows, 1), jnp.float32),
                pltpu.VMEM((head_rows, 1), jnp.float32),
                pltpu.VMEM((head_rows, RANK), jnp.float32),
            ],
        ),
        cost_estimate=pl.CostEstimate(
            flops=9_000_000_000, bytes_accessed=16_000_000, transcendentals=4_000_000
        ),
        compiler_params=pltpu.CompilerParams(
            dimension_semantics=("arbitrary",), vmem_limit_bytes=40 << 20
        ),
    )(meta, queries, qlo, qpos, *keys, w_uv)


def expert_kernel(
    order, own_ref, oth_ref, wg0, wu0, wd0, wg1, wu1, wd1, kept_ref, given_ref
):
    share = own_ref.shape[2]
    across = (((1,), (1,)), ((), ()))
    starts = [pl.multiple_of(order[j] * share, share) for j in range(4)]
    pieces = [own_ref[0], own_ref[1], oth_ref[0], oth_ref[1]]
    actives = []
    for wg_ref, wu_ref in ((wg0, wu0), (wg1, wu1)):
        gate = jnp.zeros((pieces[0].shape[0], wg_ref.shape[0]), jnp.float32)
        upper = gate
        for start, piece in zip(starts, pieces):
            gate = gate + lax.dot_general(
                piece, wg_ref[:, pl.ds(start, share)], across,
                preferred_element_type=jnp.float32,
            )
            upper = upper + lax.dot_general(
                piece, wu_ref[:, pl.ds(start, share)], across,
                preferred_element_type=jnp.float32,
            )
        actives.append((gate / (1.0 + jnp.exp(-gate)) * upper).astype(jnp.bfloat16))
    for j, start in enumerate(starts):
        parts = [
            jnp.dot(active, wd_ref[:, pl.ds(start, share)], preferred_element_type=jnp.float32)
            .astype(jnp.bfloat16)
            .astype(jnp.float32)
            for active, wd_ref in zip(actives, (wd0, wd1))
        ]
        target = kept_ref if j < 2 else given_ref
        target[j % 2] = (parts[0] + parts[1]).astype(target.dtype)


def experts(order, own, oth, *weights):
    _, count, share = own.shape
    tile = 256

    def whole(shape):
        return pl.BlockSpec(shape, lambda i, m: (0,) * len(shape))

    row_spec = pl.BlockSpec((2, tile, share), lambda i, m: (0, i, 0))
    return pl.pallas_call(
        expert_kernel,
        out_shape=[
            jax.ShapeDtypeStruct(own.shape, jnp.float32),
            jax.ShapeDtypeStruct(own.shape, jnp.bfloat16),
        ],
        grid_spec=pltpu.PrefetchScalarGridSpec(
            num_scalar_prefetch=1,
            grid=(count // tile,),
            in_specs=[row_spec] * 2 + [whole(w.shape) for w in weights],
            out_specs=[row_spec] * 2,
        ),
        cost_estimate=pl.CostEstimate(
            flops=4_400_000_000, bytes_accessed=14_000_000, transcendentals=400_000
        ),
        compiler_params=pltpu.CompilerParams(
            dimension_semantics=("arbitrary",), vmem_limit_bytes=48 << 20
        ),
    )(order, own, oth, *weights)


def layer(
    hidden, segment_ids, expert_ids, route_weight, attn_gain, kv_gain, ffn_gain,
    w_q, w_kv_a, w_kv_b, w_o, w_gate, w_up, w_down, page_table,
):
    row_count, share = hidden.shape
    yl, core = lax.axis_index("yl"), lax.axis_index("c")
    yh, x, z = (lax.axis_index(name) for name in GY)
    row_start = ((yh * XS + x) * ZS + z) * row_count
    head_count = w_q.shape[1] // (NOPE + ROPE)
    depth = w_q.shape[0]

    expand_rows = w_kv_b.shape[0]
    local_expand = (
        w_kv_b.reshape(expand_rows, head_count, NOPE + VDIM)
        .transpose(1, 0, 2)
        .reshape(expand_rows * head_count, NOPE + VDIM)
    )
    packed = jnp.concatenate([w_q, local_expand, w_o.T], axis=1)
    crowd, late = YH * XS, packed.shape[1]
    tail_cols = w_kv_a.shape[1] - 128
    latent_packed = jnp.concatenate(
        [w_kv_a[:, :128], w_kv_a[:, 128:].reshape(depth * tail_cols // 128, 128)], axis=0
    )
    latent_all = spread(latent_packed, GY, GROUPS)
    latent_main = latent_all[:, :depth].reshape(GROUPS * depth, 128)
    latent_tail = latent_all[:, depth:].reshape(GROUPS * depth, tail_cols)
    w1, w2, w3 = (shift(packed[None], "x", XS, k) for k in range(1, XS))
    circle = jnp.concatenate([w3, w2, w1, packed[None], w3, w2, w1], axis=0)
    along_x = lax.dynamic_slice_in_dim(circle, XS - 1 - x, XS)
    across_yh = swap(along_x, "yh")
    near_weights = jnp.where(
        yh == 0,
        jnp.concatenate([along_x, across_yh], axis=0),
        jnp.concatenate([across_yh, along_x], axis=0),
    )
    positions = row_start + jnp.arange(row_count, dtype=jnp.int32)
    own_segments = lax.dynamic_slice_in_dim(segment_ids, row_start, row_count)
    prompt_start = jnp.sum(
        (segment_ids[None, :] < own_segments[:, None]).astype(jnp.int32), axis=1
    )
    angles = angle_table(positions - prompt_start, ROPE)
    cosine, sine = jnp.cos(angles), jnp.sin(angles)

    full_rows = lax.all_gather(hidden, GX, axis=1, tiled=True)
    normed = norm_rows(full_rows.astype(jnp.float32), attn_gain).astype(jnp.bfloat16)

    gate_t, up_t, down = w_gate[0].T, w_up[0].T, w_down[0]
    gate_far = swap(gate_t, "yl")
    up_far = swap(up_t, "yl")
    down_far = swap(down, "yl")

    kv_part = jnp.concatenate(
        [
            jnp.dot(normed, latent_main, preferred_element_type=jnp.float32),
            jnp.dot(normed, latent_tail, preferred_element_type=jnp.float32),
        ],
        axis=1,
    )
    kv_raw = lax.all_gather(kv_part, GX, axis=1, tiled=True)
    half = row_count // CORES
    kv_half = lax.dynamic_slice_in_dim(kv_raw, core * half, half)
    keys = jnp.concatenate(
        [
            norm_rows(kv_half[:, :RANK], kv_gain),
            rotate(
                kv_half[:, RANK:],
                lax.dynamic_slice_in_dim(cosine, core * half, half),
                lax.dynamic_slice_in_dim(sine, core * half, half),
            ),
            jnp.zeros((half, WIDE - KEY), jnp.float32),
        ],
        axis=1,
    ).astype(jnp.bfloat16)
    along_z = spread(keys, "z", ZS)
    near_weights = near_weights + along_z[0, 0, 0] * 0
    front_cols = w_q.shape[1] + NOPE + VDIM
    weights = (
        lax.all_gather(
            near_weights[:, :, :front_cols].reshape(crowd * depth, front_cols), "z",
            axis=0, tiled=True,
        )
        .reshape(ZS, crowd, depth, front_cols)
        .transpose(1, 0, 2, 3)
        .reshape(GROUPS * depth, front_cols)
    )
    out_rows = lax.all_gather(
        near_weights[:, :, front_cols:].reshape(crowd * depth, late - front_cols), "z",
        axis=0, tiled=True,
    ).reshape(ZS, crowd, depth, late - front_cols)
    quarter = half // 2
    a0 = along_z[:, :quarter].reshape(1, ZS * quarter, WIDE)
    b0 = along_z[:, quarter:].reshape(1, ZS * quarter, WIDE)
    b1 = jnp.concatenate([b0, swap(b0, "yh")], axis=0)
    a1 = jnp.concatenate([a0] + [shift(a0, "x", XS, k) for k in range(1, XS)], axis=0)
    a_own = jnp.concatenate([a1, swap(a1, "yh")], axis=0)
    b_own = jnp.concatenate([b1] + [shift(b1, "x", XS, k) for k in range(1, XS)], axis=0)
    a_oth = swap(a_own, "c")
    b_oth = swap(b_own, "c")
    steps = jnp.arange(8, dtype=jnp.int32)
    base_a = ((yh ^ (steps // 4)) * XS + (x - steps % 4) % XS) * (ZS * row_count)
    base_b = ((yh ^ (steps % 2)) * XS + (x - steps // 2) % XS) * (ZS * row_count)
    meta = jnp.concatenate(
        [
            base_a, base_b,
            jnp.stack([prompt_start[0], row_start + row_count - 1, core]).astype(jnp.int32),
        ]
    ).astype(jnp.int32)

    pages = []
    for i in range(page_table.shape[0]):
        page = page_table[i]
        group, inside = page // (row_count // PAGE), page % (row_count // PAGE)
        far_yh, far_x = (group // (XS * ZS)) ^ yh, (x - (group // ZS) % XS) % XS
        start = (group % ZS) * quarter + (inside % 2) * PAGE
        is_own = inside // 4 == core
        index_a, index_b = far_yh * XS + far_x, far_x * YH + far_yh
        size = (1, PAGE, WIDE)
        from_a = jnp.where(
            is_own,
            lax.dynamic_slice(a_own, (index_a, start, 0), size),
            lax.dynamic_slice(a_oth, (index_a, start, 0), size),
        )
        from_b = jnp.where(
            is_own,
            lax.dynamic_slice(b_own, (index_b, start, 0), size),
            lax.dynamic_slice(b_oth, (index_b, start, 0), size),
        )
        pages.append(jnp.where((inside % 4) // 2 == 0, from_a, from_b))
    latent_cache = jnp.concatenate(pages, axis=0)[:, :, :KEY]

    q_cols = w_q.shape[1]
    expand = (
        weights[:, q_cols : q_cols + NOPE + VDIM]
        .reshape(GROUPS, head_count, expand_rows, NOPE + VDIM)
        .transpose(1, 0, 2, 3)
        .reshape(head_count, RANK, NOPE + VDIM)
    )
    scale = (NOPE + ROPE) ** (-0.5)
    query = jnp.dot(normed, weights[:, :q_cols], preferred_element_type=jnp.float32).reshape(
        row_count, head_count, NOPE + ROPE
    )
    q_nope = query[:, :, :NOPE].astype(jnp.bfloat16)
    absorbed = (
        jnp.einsum("thn,hrn->htr", q_nope, expand[:, :, :NOPE], preferred_element_type=jnp.float32)
        * scale
    ).astype(jnp.bfloat16)
    rotated = (
        rotate(query[:, :, NOPE:], cosine[:, None, :], sine[:, None, :]) * scale
    ).astype(jnp.bfloat16)
    blank = jnp.zeros((head_count, row_count, WIDE - KEY), jnp.bfloat16)
    queries = jnp.concatenate(
        [absorbed, jnp.transpose(rotated, (1, 0, 2)), blank], axis=2
    ).reshape(head_count * row_count, WIDE)
    qlo = jnp.tile(prompt_start.astype(jnp.int32), head_count)[:, None]
    qpos = jnp.tile(positions, head_count)[:, None]
    heads_out = attention(
        meta, queries, qlo, qpos, (a_own, a_oth, b_own, b_oth), expand[:, :, NOPE:]
    )
    head_terms = project(heads_out, out_rows)

    kept = lax.dynamic_index_in_dim(head_terms, core, 1, keepdims=False)
    given = lax.dynamic_index_in_dim(head_terms, 1 - core, 1, keepdims=False)
    pair_sum = kept + swap(given, "c")
    mine = lax.dynamic_index_in_dim(pair_sum, yl, 0, keepdims=False)
    theirs = lax.dynamic_index_in_dim(pair_sum, 1 - yl, 0, keepdims=False)
    head_sum = mine + swap(theirs, "yl")
    residual = (hidden.astype(jnp.float32) + head_sum).astype(jnp.bfloat16)
    wide = residual.astype(jnp.float32)
    squares = lax.all_gather(jnp.sum(wide * wide, axis=1)[None], GX, axis=0, tiled=True)
    mean_sq = jnp.sum(squares, axis=0)[:, None] * (1.0 / (share * PARTS))
    own_gain = lax.dynamic_slice_in_dim(ffn_gain, (yl * CORES + core) * share, share)
    ffn_in = (wide * lax.rsqrt(mean_sq + eps) * own_gain).astype(jnp.bfloat16)

    top_count = expert_ids.shape[1]
    expert_range = jnp.arange(GROUPS, dtype=jnp.int32)
    chosen = (expert_ids[:, :, None] == expert_range).astype(jnp.float32)
    named = jnp.sum(chosen, axis=1)
    earlier = (
        jnp.arange(row_count)[:, None] > jnp.arange(row_count)[None, :]
    ).astype(jnp.float32)
    before = jnp.dot(earlier, named, preferred_element_type=jnp.float32)
    ranks = jnp.sum(chosen * before[:, None, :], axis=2).astype(jnp.int32)
    slots = expert_ids * SLOTS + ranks
    order = jnp.stack([core, 2 + core, 1 - core, 3 - core]).astype(jnp.int32)
    chunk = SLOTS // YL
    group_rows = GROUPS * chunk
    counter = jnp.arange(YL * group_rows, dtype=jnp.int32)
    slot_range = counter % group_rows // chunk * SLOTS + counter % chunk + counter // group_rows * chunk
    pick = jnp.zeros((YL * group_rows, row_count), jnp.bool_)
    blend = jnp.zeros((row_count, YL * group_rows), jnp.float32)
    for k in range(top_count):
        pick = pick | (slot_range[:, None] == slots[:, k][None, :])
        blend = blend + jnp.where(
            slots[:, k][:, None] == slot_range[None, :], route_weight[:, k][:, None], 0.0
        )
    outgoing = jnp.dot(
        pick.astype(jnp.bfloat16), ffn_in, preferred_element_type=jnp.float32
    ).astype(jnp.bfloat16)
    incoming = lax.all_to_all(
        outgoing.reshape(YL * GROUPS, chunk, share), ("yl",) + GY,
        split_axis=0, concat_axis=0, tiled=True,
    ).reshape(YL, group_rows, share)
    kept, given = experts(
        order, incoming, swap(incoming, "c"), gate_t, up_t, down, gate_far, up_far, down_far
    )
    summed = (kept + swap(given, "c").astype(jnp.float32)).astype(jnp.bfloat16)
    returned = lax.all_to_all(
        summed.reshape(YL * GROUPS, chunk, share), ("yl",) + GY,
        split_axis=0, concat_axis=0, tiled=True,
    ).reshape(YL * group_rows, share)
    moe = jnp.dot(
        blend, returned.astype(jnp.float32), precision=lax.Precision.HIGHEST,
        preferred_element_type=jnp.float32,
    )
    output = (residual.astype(jnp.float32) + moe).astype(jnp.bfloat16)
    return (output, latent_cache)


def solution(mesh):
    fine = Mesh(mesh.devices.reshape(YL, CORES, YH, XS, ZS), GX + GY)
    return jax.shard_map(
        layer,
        mesh=fine,
        in_specs=(
            P(GY, GX),
            P(),
            P(GY, None),
            P(GY, None),
            P(),
            P(),
            P(),
            P(GY, GX),
            P(GY, GX),
            P(GY, GX),
            P(GX, GY),
            P(GY, None, GX),
            P(GY, None, GX),
            P(GY, GX, None),
            P(GX + GY),
        ),
        out_specs=(P(GY, GX), P(GX + GY, None, None)),
        check_vma=False,
    )
```

```python
import jax
import jax.numpy as jnp
from jax import lax
from jax.experimental import pallas as pl
from jax.experimental.pallas import tpu as pltpu
from jax.sharding import Mesh, PartitionSpec as P


NOPE = 128
ROPE = 64
VDIM = 128
RANK = 512
PAGE = 16
KEY = RANK + ROPE
WIDE = 640

GX = ("yl", "c")
GY = ("yh", "x", "z")
YL, CORES, YH, XS, ZS = 2, 2, 2, 4, 8
GROUPS = YH * XS * ZS
PARTS = YL * CORES
SLOTS = 16
SWAP = [(0, 1), (1, 0)]

eps = 1e-06
masked_score = -1e30


def norm_rows(values, gain):
    mean_sq = jnp.mean(values * values, axis=-1, keepdims=True)
    return values * lax.rsqrt(mean_sq + eps) * gain


def angle_table(positions, width):
    exponents = jnp.arange(width // 2, dtype=jnp.float32) * (2.0 / width)
    freqs = jnp.power(10000.0, -exponents)
    return positions.astype(jnp.float32)[:, None] * freqs[None, :]


def rotate(values, cosine, sine):
    half = values.shape[-1] // 2
    first = values[..., :half]
    second = values[..., half:]
    return jnp.concatenate(
        [first * cosine - second * sine, second * cosine + first * sine], axis=-1
    )


def shift(values, axis, size, step):
    return lax.ppermute(values, axis, [(i, (i + step) % size) for i in range(size)])


def swap(values, axis):
    return lax.ppermute(values, axis, SWAP)


def spread(values, axis, size):
    blocks = jnp.broadcast_to(values[None], (size,) + values.shape)
    return lax.all_to_all(blocks, axis, split_axis=0, concat_axis=0, tiled=True)


def attention_kernel(
    meta, q_ref, qlo_ref, qpos_ref, a_own, a_oth, b_own, b_oth, wuv_ref, out_ref,
    best, total, accum,
):
    step = pl.program_id(0)
    kmin, kmax, core = meta[16], meta[17], meta[18]

    @pl.when(step == 0)
    def _():
        best[...] = jnp.full_like(best, masked_score)
        total[...] = jnp.zeros_like(total)
        accum[...] = jnp.zeros_like(accum)

    def block(base, colour, own_ref, oth_ref):
        @pl.when((base <= kmax) & (base + 1023 >= kmin))
        def _():
            queries = q_ref[...]
            lo, hi = qlo_ref[...], qpos_ref[...]
            row = lax.broadcasted_iota(jnp.int32, (1, 256), 1)
            place = base + (row // 32) * 128 + row % 32 + colour * 32
            scores, masks = [], []
            for ref, side in ((own_ref, core), (oth_ref, 1 - core)):
                keys = ref[0]
                raw = lax.dot_general(
                    queries, keys, (((1,), (1,)), ((), ())), preferred_element_type=jnp.float32
                )
                where = place + side * 64
                mask = (where >= lo) & (where <= hi)
                scores.append(jnp.where(mask, raw, masked_score))
                masks.append(mask)
            old = best[...]
            new = jnp.maximum(
                old,
                jnp.maximum(
                    jnp.max(scores[0], axis=-1, keepdims=True),
                    jnp.max(scores[1], axis=-1, keepdims=True),
                ),
            )
            alpha = jnp.exp(old - new)
            best[...] = new
            grown = total[...] * alpha
            fresh = accum[...] * alpha
            for ref, score, mask in ((own_ref, scores[0], masks[0]), (oth_ref, scores[1], masks[1])):
                weight = jnp.where(mask, jnp.exp(score - new), 0.0)
                grown = grown + jnp.sum(weight, axis=-1, keepdims=True)
                fresh = fresh + jnp.dot(
                    weight.astype(jnp.bfloat16), ref[0, :, :RANK],
                    preferred_element_type=jnp.float32,
                )
            total[...] = grown
            accum[...] = fresh

    block(meta[step], 0, a_own, a_oth)
    block(meta[8 + step], 1, b_own, b_oth)

    @pl.when(step == pl.num_programs(0) - 1)
    def _():
        rows = out_ref.shape[0]
        mixed = (accum[...] / total[...]).astype(jnp.bfloat16)
        for h in range(wuv_ref.shape[0]):
            out_ref[:, h * VDIM : (h + 1) * VDIM] = jnp.dot(
                mixed[h * rows : (h + 1) * rows], wuv_ref[h], preferred_element_type=jnp.float32
            ).astype(jnp.bfloat16)


def project_kernel(heads_ref, wo_ref, out_ref):
    heads = heads_ref[...]
    crowds = wo_ref.shape[1] // PARTS
    for part in range(PARTS):
        rows = jnp.concatenate(
            [
                wo_ref[z, part * crowds + j]
                for j in range(crowds)
                for z in range(wo_ref.shape[0])
            ],
            axis=0,
        )
        out_ref[part // CORES, part % CORES] = lax.dot_general(
            heads, rows, (((1,), (1,)), ((), ())), preferred_element_type=jnp.float32
        )


def project(heads_out, out_rows):
    zs, crowd, depth, _ = out_rows.shape
    width = zs * crowd * depth // PARTS
    return pl.pallas_call(
        project_kernel,
        out_shape=jax.ShapeDtypeStruct(
            (YL, CORES, heads_out.shape[0], width), jnp.float32
        ),
        in_specs=[pl.BlockSpec(memory_space=pltpu.VMEM)] * 2,
        out_specs=pl.BlockSpec(memory_space=pltpu.VMEM),
        cost_estimate=pl.CostEstimate(
            flops=270_000_000, bytes_accessed=3_000_000, transcendentals=0
        ),
        compiler_params=pltpu.CompilerParams(vmem_limit_bytes=24 << 20),
    )(heads_out, out_rows)


def attention(meta, queries, qlo, qpos, keys, w_uv):
    head_rows = queries.shape[0]
    rows = head_rows // w_uv.shape[0]
    out_dims = (rows, w_uv.shape[0] * VDIM)

    def whole(shape):
        return pl.BlockSpec(shape, lambda i, m: (0,) * len(shape))

    key_spec = pl.BlockSpec((1, 256, WIDE), lambda i, m: (i, 0, 0))
    return pl.pallas_call(
        attention_kernel,
        out_shape=jax.ShapeDtypeStruct(out_dims, jnp.bfloat16),
        grid_spec=pltpu.PrefetchScalarGridSpec(
            num_scalar_prefetch=1,
            grid=(8,),
            in_specs=[
                whole(queries.shape), whole(qlo.shape), whole(qpos.shape),
                key_spec, key_spec, key_spec, key_spec,
                whole(w_uv.shape),
            ],
            out_specs=whole(out_dims),
            scratch_shapes=[
                pltpu.VMEM((head_rows, 1), jnp.float32),
                pltpu.VMEM((head_rows, 1), jnp.float32),
                pltpu.VMEM((head_rows, RANK), jnp.float32),
            ],
        ),
        cost_estimate=pl.CostEstimate(
            flops=9_000_000_000, bytes_accessed=16_000_000, transcendentals=4_000_000
        ),
        compiler_params=pltpu.CompilerParams(
            dimension_semantics=("arbitrary",), vmem_limit_bytes=40 << 20
        ),
    )(meta, queries, qlo, qpos, *keys, w_uv)


def expert_kernel(
    order, own_ref, oth_ref, wg0, wu0, wd0, wg1, wu1, wd1, kept_ref, given_ref
):
    share = own_ref.shape[2]
    across = (((1,), (1,)), ((), ()))
    starts = [pl.multiple_of(order[j] * share, share) for j in range(4)]
    pieces = [own_ref[0], own_ref[1], oth_ref[0], oth_ref[1]]
    actives = []
    for wg_ref, wu_ref in ((wg0, wu0), (wg1, wu1)):
        gate = jnp.zeros((pieces[0].shape[0], wg_ref.shape[0]), jnp.float32)
        upper = gate
        for start, piece in zip(starts, pieces):
            gate = gate + lax.dot_general(
                piece, wg_ref[:, pl.ds(start, share)], across,
                preferred_element_type=jnp.float32,
            )
            upper = upper + lax.dot_general(
                piece, wu_ref[:, pl.ds(start, share)], across,
                preferred_element_type=jnp.float32,
            )
        actives.append((gate / (1.0 + jnp.exp(-gate)) * upper).astype(jnp.bfloat16))
    for j, start in enumerate(starts):
        parts = [
            jnp.dot(active, wd_ref[:, pl.ds(start, share)], preferred_element_type=jnp.float32)
            .astype(jnp.bfloat16)
            .astype(jnp.float32)
            for active, wd_ref in zip(actives, (wd0, wd1))
        ]
        target = kept_ref if j < 2 else given_ref
        target[j % 2] = (parts[0] + parts[1]).astype(target.dtype)


def experts(order, own, oth, *weights):
    _, count, share = own.shape
    tile = 256

    def whole(shape):
        return pl.BlockSpec(shape, lambda i, m: (0,) * len(shape))

    row_spec = pl.BlockSpec((2, tile, share), lambda i, m: (0, i, 0))
    return pl.pallas_call(
        expert_kernel,
        out_shape=[
            jax.ShapeDtypeStruct(own.shape, jnp.float32),
            jax.ShapeDtypeStruct(own.shape, jnp.bfloat16),
        ],
        grid_spec=pltpu.PrefetchScalarGridSpec(
            num_scalar_prefetch=1,
            grid=(count // tile,),
            in_specs=[row_spec] * 2 + [whole(w.shape) for w in weights],
            out_specs=[row_spec] * 2,
        ),
        cost_estimate=pl.CostEstimate(
            flops=4_400_000_000, bytes_accessed=14_000_000, transcendentals=400_000
        ),
        compiler_params=pltpu.CompilerParams(
            dimension_semantics=("arbitrary",), vmem_limit_bytes=48 << 20
        ),
    )(order, own, oth, *weights)


def layer(
    hidden, segment_ids, expert_ids, route_weight, attn_gain, kv_gain, ffn_gain,
    w_q, w_kv_a, w_kv_b, w_o, w_gate, w_up, w_down, page_table,
):
    row_count, share = hidden.shape
    yl, core = lax.axis_index("yl"), lax.axis_index("c")
    yh, x, z = (lax.axis_index(name) for name in GY)
    row_start = ((yh * XS + x) * ZS + z) * row_count
    head_count = w_q.shape[1] // (NOPE + ROPE)
    depth = w_q.shape[0]

    expand_rows = w_kv_b.shape[0]
    local_expand = (
        w_kv_b.reshape(expand_rows, head_count, NOPE + VDIM)
        .transpose(1, 0, 2)
        .reshape(expand_rows * head_count, NOPE + VDIM)
    )
    packed = jnp.concatenate([w_q, local_expand, w_o.T], axis=1)
    crowd, late = YH * XS, packed.shape[1]
    tail_cols = w_kv_a.shape[1] - 128
    latent_packed = jnp.concatenate(
        [w_kv_a[:, :128], w_kv_a[:, 128:].reshape(depth * tail_cols // 128, 128)], axis=0
    )
    latent_all = spread(latent_packed, GY, GROUPS)
    latent_main = latent_all[:, :depth].reshape(GROUPS * depth, 128)
    latent_tail = latent_all[:, depth:].reshape(GROUPS * depth, tail_cols)
    w1, w2, w3 = (shift(packed[None], "x", XS, k) for k in range(1, XS))
    circle = jnp.concatenate([w3, w2, w1, packed[None], w3, w2, w1], axis=0)
    along_x = lax.dynamic_slice_in_dim(circle, XS - 1 - x, XS)
    across_yh = swap(along_x, "yh")
    near_weights = jnp.where(
        yh == 0,
        jnp.concatenate([along_x, across_yh], axis=0),
        jnp.concatenate([across_yh, along_x], axis=0),
    )
    positions = row_start + jnp.arange(row_count, dtype=jnp.int32)
    own_segments = lax.dynamic_slice_in_dim(segment_ids, row_start, row_count)
    prompt_start = jnp.sum(
        (segment_ids[None, :] < own_segments[:, None]).astype(jnp.int32), axis=1
    )
    angles = angle_table(positions - prompt_start, ROPE)
    cosine, sine = jnp.cos(angles), jnp.sin(angles)

    full_rows = lax.all_gather(hidden, GX, axis=1, tiled=True)
    normed = norm_rows(full_rows.astype(jnp.float32), attn_gain).astype(jnp.bfloat16)

    gate_t, up_t, down = w_gate[0].T, w_up[0].T, w_down[0]
    gate_far = swap(gate_t, "yl")
    up_far = swap(up_t, "yl")
    down_far = swap(down, "yl")

    kv_part = jnp.concatenate(
        [
            jnp.dot(normed, latent_main, preferred_element_type=jnp.float32),
            jnp.dot(normed, latent_tail, preferred_element_type=jnp.float32),
        ],
        axis=1,
    )
    kv_raw = lax.all_gather(kv_part, GX, axis=1, tiled=True)
    half = row_count // CORES
    kv_half = lax.dynamic_slice_in_dim(kv_raw, core * half, half)
    keys = jnp.concatenate(
        [
            norm_rows(kv_half[:, :RANK], kv_gain),
            rotate(
                kv_half[:, RANK:],
                lax.dynamic_slice_in_dim(cosine, core * half, half),
                lax.dynamic_slice_in_dim(sine, core * half, half),
            ),
            jnp.zeros((half, WIDE - KEY), jnp.float32),
        ],
        axis=1,
    ).astype(jnp.bfloat16)
    along_z = spread(keys, "z", ZS)
    near_weights = near_weights + along_z[0, 0, 0] * 0
    front_cols = w_q.shape[1] + NOPE + VDIM
    weights = (
        lax.all_gather(
            near_weights[:, :, :front_cols].reshape(crowd * depth, front_cols), "z",
            axis=0, tiled=True,
        )
        .reshape(ZS, crowd, depth, front_cols)
        .transpose(1, 0, 2, 3)
        .reshape(GROUPS * depth, front_cols)
    )
    out_rows = lax.all_gather(
        near_weights[:, :, front_cols:].reshape(crowd * depth, late - front_cols), "z",
        axis=0, tiled=True,
    ).reshape(ZS, crowd, depth, late - front_cols)
    quarter = half // 2
    a0 = along_z[:, :quarter].reshape(1, ZS * quarter, WIDE)
    b0 = along_z[:, quarter:].reshape(1, ZS * quarter, WIDE)
    b0_far = swap(b0, "yh")
    b1 = jnp.concatenate([b0, b0_far], axis=0)
    a1 = jnp.concatenate([a0] + [shift(a0, "x", XS, k) for k in range(1, XS)], axis=0)
    a1_far = swap(a1, "yh")
    a_own = jnp.concatenate([a1, a1_far], axis=0)
    b_own = jnp.concatenate([b1] + [shift(b1, "x", XS, k) for k in range(1, XS)], axis=0)
    a_oth = swap(a_own, "c")
    b_oth = swap(b_own, "c")
    steps = jnp.arange(8, dtype=jnp.int32)
    base_a = ((yh ^ (steps // 4)) * XS + (x - steps % 4) % XS) * (ZS * row_count)
    base_b = ((yh ^ (steps % 2)) * XS + (x - steps // 2) % XS) * (ZS * row_count)
    meta = jnp.concatenate(
        [
            base_a, base_b,
            jnp.stack([prompt_start[0], row_start + row_count - 1, core]).astype(jnp.int32),
        ]
    ).astype(jnp.int32)

    pages = []
    for i in range(page_table.shape[0]):
        page = page_table[i]
        group, inside = page // (row_count // PAGE), page % (row_count // PAGE)
        far_yh, far_x = (group // (XS * ZS)) ^ yh, (x - (group // ZS) % XS) % XS
        start = (group % ZS) * quarter + (inside % 2) * PAGE
        is_own = inside // 4 == core
        index_a, index_b = far_yh * XS + far_x, far_x * YH + far_yh
        size = (1, PAGE, WIDE)
        from_a = jnp.where(
            is_own,
            lax.dynamic_slice(a_own, (index_a, start, 0), size),
            lax.dynamic_slice(a_oth, (index_a, start, 0), size),
        )
        from_b = jnp.where(
            is_own,
            lax.dynamic_slice(b_own, (index_b, start, 0), size),
            lax.dynamic_slice(b_oth, (index_b, start, 0), size),
        )
        pages.append(jnp.where((inside % 4) // 2 == 0, from_a, from_b))
    latent_cache = jnp.concatenate(pages, axis=0)[:, :, :KEY]

    q_cols = w_q.shape[1]
    expand = (
        weights[:, q_cols : q_cols + NOPE + VDIM]
        .reshape(GROUPS, head_count, expand_rows, NOPE + VDIM)
        .transpose(1, 0, 2, 3)
        .reshape(head_count, RANK, NOPE + VDIM)
    )
    scale = (NOPE + ROPE) ** (-0.5)
    query = jnp.dot(normed, weights[:, :q_cols], preferred_element_type=jnp.float32).reshape(
        row_count, head_count, NOPE + ROPE
    )
    q_nope = query[:, :, :NOPE].astype(jnp.bfloat16)
    absorbed = (
        jnp.einsum("thn,hrn->htr", q_nope, expand[:, :, :NOPE], preferred_element_type=jnp.float32)
        * scale
    ).astype(jnp.bfloat16)
    rotated = (
        rotate(query[:, :, NOPE:], cosine[:, None, :], sine[:, None, :]) * scale
    ).astype(jnp.bfloat16)
    blank = jnp.zeros((head_count, row_count, WIDE - KEY), jnp.bfloat16)
    queries = jnp.concatenate(
        [absorbed, jnp.transpose(rotated, (1, 0, 2)), blank], axis=2
    ).reshape(head_count * row_count, WIDE)
    qlo = jnp.tile(prompt_start.astype(jnp.int32), head_count)[:, None]
    qpos = jnp.tile(positions, head_count)[:, None]
    heads_out = attention(
        meta, queries, qlo, qpos, (a_own, a_oth, b_own, b_oth), expand[:, :, NOPE:]
    )
    head_terms = project(heads_out, out_rows)

    kept = lax.dynamic_index_in_dim(head_terms, core, 1, keepdims=False)
    given = lax.dynamic_index_in_dim(head_terms, 1 - core, 1, keepdims=False)
    pair_sum = kept + swap(given, "c")
    mine = lax.dynamic_index_in_dim(pair_sum, yl, 0, keepdims=False)
    theirs = lax.dynamic_index_in_dim(pair_sum, 1 - yl, 0, keepdims=False)
    head_sum = mine + swap(theirs, "yl")
    residual = (hidden.astype(jnp.float32) + head_sum).astype(jnp.bfloat16)
    wide = residual.astype(jnp.float32)
    squares = lax.all_gather(jnp.sum(wide * wide, axis=1)[None], GX, axis=0, tiled=True)
    mean_sq = jnp.sum(squares, axis=0)[:, None] * (1.0 / (share * PARTS))
    own_gain = lax.dynamic_slice_in_dim(ffn_gain, (yl * CORES + core) * share, share)
    ffn_in = (wide * lax.rsqrt(mean_sq + eps) * own_gain).astype(jnp.bfloat16)

    top_count = expert_ids.shape[1]
    expert_range = jnp.arange(GROUPS, dtype=jnp.int32)
    chosen = (expert_ids[:, :, None] == expert_range).astype(jnp.float32)
    named = jnp.sum(chosen, axis=1)
    earlier = (
        jnp.arange(row_count)[:, None] > jnp.arange(row_count)[None, :]
    ).astype(jnp.float32)
    before = jnp.dot(earlier, named, preferred_element_type=jnp.float32)
    ranks = jnp.sum(chosen * before[:, None, :], axis=2).astype(jnp.int32)
    slots = expert_ids * SLOTS + ranks
    order = jnp.stack([core, 2 + core, 1 - core, 3 - core]).astype(jnp.int32)
    chunk = SLOTS // YL
    group_rows = GROUPS * chunk
    counter = jnp.arange(YL * group_rows, dtype=jnp.int32)
    slot_range = counter % group_rows // chunk * SLOTS + counter % chunk + counter // group_rows * chunk
    pick = jnp.zeros((YL * group_rows, row_count), jnp.bool_)
    blend = jnp.zeros((row_count, YL * group_rows), jnp.float32)
    for k in range(top_count):
        pick = pick | (slot_range[:, None] == slots[:, k][None, :])
        blend = blend + jnp.where(
            slots[:, k][:, None] == slot_range[None, :], route_weight[:, k][:, None], 0.0
        )
    outgoing = jnp.dot(
        pick.astype(jnp.bfloat16), ffn_in, preferred_element_type=jnp.float32
    ).astype(jnp.bfloat16)
    incoming = lax.all_to_all(
        outgoing.reshape(YL * GROUPS, chunk, share), ("yl",) + GY,
        split_axis=0, concat_axis=0, tiled=True,
    )
    incoming = incoming.reshape(YL, group_rows, share)
    kept, given = experts(
        order, incoming, swap(incoming, "c"), gate_t, up_t, down, gate_far, up_far, down_far
    )
    summed = (kept + swap(given, "c").astype(jnp.float32)).astype(jnp.bfloat16)
    returned = lax.all_to_all(
        summed.reshape(YL * GROUPS, chunk, share), ("yl",) + GY,
        split_axis=0, concat_axis=0, tiled=True,
    ).reshape(YL * group_rows, share)
    moe = jnp.dot(
        blend, returned.astype(jnp.float32), precision=lax.Precision.HIGHEST,
        preferred_element_type=jnp.float32,
    )
    output = (residual.astype(jnp.float32) + moe).astype(jnp.bfloat16)
    return (output, latent_cache)


def solution(mesh):
    fine = Mesh(mesh.devices.reshape(YL, CORES, YH, XS, ZS), GX + GY)
    return jax.shard_map(
        layer,
        mesh=fine,
        in_specs=(
            P(GY, GX),
            P(),
            P(GY, None),
            P(GY, None),
            P(),
            P(),
            P(),
            P(GY, GX),
            P(GY, GX),
            P(GY, GX),
            P(GX, GY),
            P(GY, None, GX),
            P(GY, None, GX),
            P(GY, GX, None),
            P(GX + GY),
        ),
        out_specs=(P(GY, GX), P(GX + GY, None, None)),
        check_vma=False,
    )
```
